32 devices in a mesh: groups: 2 (over y), db: 4 (over x, core), cand: 4 (over z).
Axes of the slice: x: 2, y: 2, z: 4, core: 2. Of those that a mesh axis runs over, the one named last changes fastest.
Arguments:
- coords: float32 [3, 128, 64], P(None, ('groups', 'db', 'cand')), parts along dimension 1, may hold values from 0 to 1
- species: int32 [128, 64], P(('groups', 'db', 'cand')), parts along dimension 0, may hold values from 0 to 88
- miller: int32 [3, 4096], replicated, may hold values from -8 to 8
- offsets: int32 [4096], replicated, may hold values from 0 to 1023
- form_amps: float32 [89, 4], replicated, may hold values from 0.5 to 6
- form_decay: float32 [89, 4], replicated, may hold values from 0.2 to 20
- ref_patterns: bfloat16 [65536, 1024], P(('db', 'cand')), may hold values from -6 to 6
Outputs:
- scores: bfloat16 [128, 65536], P('groups', ('db', 'cand')), parts along dimension 0
The draws below stay inside these ranges and needn't reach their ends.
There are 2 independent parts, one for each index of `groups`. The reference program is written for one: setup_inputs(seed, part) draws one part's arguments, and reference() takes and returns one part's arrays. A program takes and returns all parts, laid end to end along the dimension named above; an argument that names none is the same for every part. Nothing has to cross between parts.
All inputs are finite; a program needn't handle non-finite values.
Results may differ from the reference program's by a relative error of at most 0.0071.
Values may be sent and summed in bfloat16 or wider, within the bound.
No kernel may reach another device: no remote copies, remote signals or barrier semaphores. Data moves between devices by JAX's collectives and lax.ppermute only.
A program may use at most 64 MiB of HBM per device.

```python
import math
import jax
import jax.numpy as jnp
from jax import lax

A = 64
S = 89
R = 4096
B = 1024
CAND_DEV = 4
REF_DEV = 4096
C = 64
NREF = 65536
N_CAND = 4


def touch_ends(values, rng, smallest, high):
    shape = values.shape
    spot = [jax.random.randint(jax.random.fold_in(rng, axis), (), 0, shape[axis]) for axis in range(len(shape))]
    values = values.at[tuple(spot)].set(smallest)
    longest = shape.index(max(shape))
    spot[longest] = (spot[longest] + 1) % shape[longest]
    return values.at[tuple(spot)].set(high)


def level_of(own_key, extent, split, smallest, top_value):
    loudness = 1.0
    for axis_at, shards_of in split:
        heights = jax.random.uniform(jax.random.fold_in(jax.random.fold_in(own_key, 6), axis_at), (shards_of,), jnp.float32, smallest / len(split), top_value / len(split))
        loudness = loudness * jnp.repeat(jnp.exp(heights), extent[axis_at] // shards_of).reshape((-1,) + (1,) * (len(extent) - 1 - axis_at))
    return loudness


def bell_draw(own_key, dims, scale, most, shards=(), kind=jnp.bfloat16):
    array = jax.random.normal(own_key, dims, jnp.float32) * scale
    if len(shards) > 0:
        array = level_of(own_key, dims, shards, -0.22, 0.18) * array
    return jnp.clip(array, min=-most, max=most).astype(kind)


def setup_inputs(seed: int = 0, part: int = 0) -> dict:
    keys = jax.random.split(jax.random.key(seed), 8)
    own_keys = jax.random.split(jax.random.fold_in(keys[7], part), 8)
    return {
        "coords": jnp.clip(1.0 * jax.random.uniform(own_keys[0], (3, C, A), jnp.float32) ** level_of(own_keys[0], (3, C, A), ((1, 16),), -0.2, 0.2), 0.0, 1.0),
        "species": touch_ends(jax.random.randint(own_keys[1], (C, A), 0, S), jax.random.fold_in(own_keys[1], 1), 0, S - 1).astype(jnp.int32),
        "miller": touch_ends(jax.random.randint(keys[2], (3, R), -8, 9), jax.random.fold_in(keys[2], 1), -8, 8).astype(jnp.int32),
        "offsets": touch_ends(jax.random.randint(keys[3], (R,), 0, B), jax.random.fold_in(keys[3], 1), 0, B - 1).astype(jnp.int32),
        "form_amps": jnp.clip(jnp.exp(jax.random.uniform(keys[4], (S, 4), jnp.float32, math.log(0.5), math.log(6.0))), 0.5, 6.0),
        "form_decay": jnp.clip(jnp.exp(jax.random.uniform(keys[5], (S, 4), jnp.float32, math.log(0.2), math.log(20.0))), 0.2, 20.0),
        "ref_patterns": bell_draw(keys[6], (NREF, B), 1.0, 6.0, ((0, 16),)),
    }


EPSILON = 1e-06
Q_SCALE = 0.0025
PEAK_WIDTH = 0.5
TWO_PI = 6.283185307179586

def form_table(indices, form_amps, form_decay):
    q_square = (indices[0] * indices[0] + indices[1] * indices[1] + indices[2] * indices[2]) * Q_SCALE
    result = jnp.zeros((form_amps.shape[0], indices.shape[1]), jnp.float32)
    for term in range(4):
        result = result + form_amps[:, term:term + 1] * jnp.exp(-form_decay[:, term:term + 1] * q_square[None, :])
    return result.astype(jnp.bfloat16)

def standardize(rows):
    row_mean = lax.optimization_barrier(jnp.mean(rows, axis=1, keepdims=True))
    centered = rows - row_mean
    spread = jnp.sqrt(lax.optimization_barrier(jnp.mean(centered * centered, axis=1, keepdims=True)) + EPSILON)
    return (centered / spread).astype(jnp.bfloat16)

def reference(coords, species, miller, offsets, form_amps, form_decay, ref_patterns):
    indices = miller.astype(jnp.float32)
    centres = offsets.astype(jnp.float32)
    table = form_table(indices, form_amps, form_decay)
    bin_grid = jnp.arange(B, dtype=jnp.float32)
    distance = (bin_grid[None, :] - centres[:, None]) / PEAK_WIDTH
    profile = jnp.exp(-0.5 * distance * distance).astype(jnp.bfloat16)
    group = CAND_DEV * N_CAND
    nblock = C // group
    coord_blocks = jnp.transpose(coords.reshape(3, nblock, group, A), (1, 0, 2, 3))
    species_blocks = species.reshape(nblock, group, A).astype(jnp.float32)
    kinds = jnp.arange(S, dtype=jnp.float32)

    def one_block(items):
        block_coords, block_species = items
        onehot = (block_species.reshape(-1)[:, None] == kinds[None, :]).astype(jnp.bfloat16)
        weights = jnp.dot(onehot, table, preferred_element_type=jnp.float32).reshape(group, A, R)
        phases = TWO_PI * (block_coords[0][:, :, None] * indices[0][None, None, :] + block_coords[1][:, :, None] * indices[1][None, None, :] + block_coords[2][:, :, None] * indices[2][None, None, :])
        real_part = lax.optimization_barrier(jnp.sum(weights * jnp.cos(phases), axis=1))
        imag_part = lax.optimization_barrier(jnp.sum(weights * jnp.sin(phases), axis=1))
        intensity = (real_part * real_part + imag_part * imag_part).astype(jnp.bfloat16)
        return jnp.dot(intensity, profile, preferred_element_type=jnp.float32)
    pattern = lax.map(one_block, (coord_blocks, species_blocks)).reshape(C, B)
    cand_z = standardize(pattern)
    scale_back = 1.0 / jnp.sqrt(jnp.float32(B))
    nref_blocks = NREF // REF_DEV
    ref_blocks = ref_patterns.reshape(nref_blocks, REF_DEV, B)

    def one_slab(slab):
        ref_z = standardize(slab.astype(jnp.float32))
        product = lax.dot_general(cand_z, ref_z, (((1,), (1,)), ((), ())), preferred_element_type=jnp.float32)
        return (product * scale_back).astype(jnp.bfloat16)
    slabs = lax.map(one_slab, ref_blocks)
    return jnp.transpose(slabs, (1, 0, 2)).reshape(C, NREF)
```

```python
import functools

import jax
import jax.numpy as jnp
from jax import lax
from jax.experimental import pallas as pl
from jax.experimental.pallas import tpu as pltpu
from jax.sharding import PartitionSpec as P

EPSILON = 1e-06
Q_SCALE = 0.0025
PEAK_WIDTH = 0.5
LANES = 128
NORMS = 256
CHUNK = 512
REF_ROWS = 512

SIN_COEFS = (3.14159258, -5.1677069, 2.55003164, -0.59804645, 0.07722225)
COS_COEFS = (0.99999995, -4.93479286, 4.05841191, -1.33188016, 0.21969679)


def horner(coefs, x):
    result = coefs[-1] * x + coefs[-2]
    for coef in coefs[-3::-1]:
        result = result * x + coef
    return result


def flat_lanes(rows):
    return jnp.concatenate([rows[c : c + 1] for c in range(rows.shape[0])], axis=1)


def candidate_kernel(
    coords_ref, species_ref, miller_ref, offsets_ref, amps_ref, decay_ref, out_ref,
    places_ref, table_ref, spread_ref,
):
    f32, bf16 = jnp.float32, jnp.bfloat16
    count, atoms = species_ref.shape
    kinds = amps_ref.shape[1]
    reflections = miller_ref.shape[1]
    nbins = out_ref.shape[1]
    nblocks = nbins // LANES
    flat = count * atoms

    pieces = []
    for axis in range(3):
        value = flat_lanes(coords_ref[axis])
        for _ in range(3):
            piece = value.astype(bf16)
            value = value - piece.astype(f32)
            pieces.append(piece.astype(f32))
    places_ref[...] = jnp.concatenate(pieces, axis=0).astype(bf16).T

    norms = lax.broadcasted_iota(jnp.int32, (NORMS, kinds), 0).astype(f32) * Q_SCALE
    table = jnp.zeros((NORMS, kinds), f32)
    for term in range(amps_ref.shape[0]):
        table = table + amps_ref[term : term + 1, :] * jnp.exp(
            -decay_ref[term : term + 1, :] * norms
        )
    onehot = (
        lax.broadcasted_iota(jnp.int32, (kinds, flat), 0) == flat_lanes(species_ref[...])
    ).astype(f32).astype(bf16)
    table_ref[...] = jnp.dot(
        table.astype(bf16), onehot, preferred_element_type=f32
    ).astype(bf16).T

    spread_ref[...] = jnp.zeros_like(spread_ref)

    def step(index, carry):
        cols = pl.ds(pl.multiple_of(index * CHUNK, CHUNK), CHUNK)
        miller = miller_ref[:, cols]
        norm = jnp.sum(miller * miller, axis=0, keepdims=True)
        hkl = miller.astype(f32)
        hkl9 = jnp.concatenate(
            [hkl[axis : axis + 1] for axis in range(3) for _ in range(3)], axis=0
        ).astype(bf16)
        turns = jnp.dot(places_ref[...], hkl9, preferred_element_type=f32)
        pick = (
            lax.broadcasted_iota(jnp.int32, (NORMS, CHUNK), 0) == norm
        ).astype(f32).astype(bf16)
        weight = jnp.dot(table_ref[...], pick, preferred_element_type=f32)
        u = turns - jnp.round(turns)
        square = u * u
        half_sin = u * horner(SIN_COEFS, square)
        half_cos = horner(COS_COEFS, square)
        part = weight * half_sin
        total = jnp.sum(weight.reshape(count, atoms, CHUNK), axis=1)
        real = total - 2.0 * jnp.sum((part * half_sin).reshape(count, atoms, CHUNK), axis=1)
        imag = 2.0 * jnp.sum((part * half_cos).reshape(count, atoms, CHUNK), axis=1)
        intensity = (real * real + imag * imag).astype(bf16).astype(f32)

        offset = offsets_ref[:, cols]
        block = offset // LANES
        local = (offset - block * LANES).astype(f32)
        routed = jnp.concatenate(
            [jnp.where(block == i, intensity, 0.0) for i in range(nblocks)], axis=0
        ).astype(bf16)
        bins = lax.broadcasted_iota(jnp.int32, (2 * LANES, CHUNK), 0)
        bins = jnp.where(bins < LANES + LANES // 2, bins, bins - 2 * LANES).astype(f32)
        distance = (bins - local) * (1.0 / PEAK_WIDTH)
        profile = jnp.exp(-0.5 * distance * distance).astype(bf16)
        spread_ref[...] += lax.dot_general(
            routed, profile, (((1,), (1,)), ((), ())), preferred_element_type=f32
        )
        return carry

    lax.fori_loop(0, reflections // CHUNK, step, 0)

    lane = lax.broadcasted_iota(jnp.int32, (count, LANES), 1)
    blocks = []
    for i in range(nblocks):
        own = spread_ref[i * count : (i + 1) * count, :LANES]
        before = after = jnp.zeros_like(own)
        if i > 0:
            before = spread_ref[(i - 1) * count : i * count, LANES:]
        if i + 1 < nblocks:
            after = spread_ref[(i + 1) * count : (i + 2) * count, LANES:]
        blocks.append(own + jnp.where(lane < LANES // 2, before, after))
    pattern = jnp.concatenate(blocks, axis=1)
    centered = pattern - jnp.mean(pattern, axis=1, keepdims=True)
    variance = jnp.mean(centered * centered, axis=1, keepdims=True)
    out_ref[...] = (centered / jnp.sqrt(variance + EPSILON)).astype(bf16)


def candidate_patterns(coords, species, miller, offsets, form_amps, form_decay, nbins):
    count, atoms = species.shape
    return pl.pallas_call(
        candidate_kernel,
        out_shape=jax.ShapeDtypeStruct((count, nbins), jnp.bfloat16),
        scratch_shapes=[
            pltpu.VMEM((count * atoms, 9), jnp.bfloat16),
            pltpu.VMEM((count * atoms, NORMS), jnp.bfloat16),
            pltpu.VMEM((count * (nbins // LANES), 2 * LANES), jnp.float32),
        ],
        name="candidates",
    )(coords, species, miller, offsets[None, :], form_amps.T, form_decay.T)


def standardize_kernel(rows_ref, out_ref):
    rows = rows_ref[...].astype(jnp.float32)
    centered = rows - jnp.mean(rows, axis=1, keepdims=True)
    variance = jnp.mean(centered * centered, axis=1, keepdims=True)
    out_ref[...] = (centered * lax.rsqrt(variance + EPSILON)).astype(jnp.bfloat16)


def standardize_refs(rows):
    count, nbins = rows.shape
    spec = pl.BlockSpec((REF_ROWS, nbins), lambda i: (i, 0))
    return pl.pallas_call(
        standardize_kernel,
        out_shape=jax.ShapeDtypeStruct(rows.shape, jnp.bfloat16),
        grid=(count // REF_ROWS,),
        in_specs=[spec],
        out_specs=spec,
        cost_estimate=pl.CostEstimate(
            flops=6 * count * nbins, bytes_accessed=4 * count * nbins, transcendentals=0
        ),
        name="references",
    )(rows)


def score_kernel(masks, position_ref, cand_ref, refs_ref, out_ref, sorted_ref):
    total = cand_ref.shape[0]
    block = total // 2 ** len(masks)

    @pl.when(pl.program_id(0) == 0)
    def _():
        place = lax.broadcasted_iota(jnp.int32, (total, total), 1)
        group = place // block
        source = jnp.full_like(group, position_ref[0])
        for bit, mask in enumerate(masks):
            source = source ^ jnp.where((group >> bit) % 2 == 1, mask, 0)
        wanted = source * block + place % block
        row = lax.broadcasted_iota(jnp.int32, (total, total), 0)
        order = (row == wanted).astype(jnp.float32).astype(jnp.bfloat16)
        sorted_ref[...] = jnp.dot(
            order, cand_ref[...], preferred_element_type=jnp.float32
        ).astype(jnp.bfloat16)

    product = lax.dot_general(
        sorted_ref[...],
        refs_ref[...],
        (((1,), (1,)), ((), ())),
        preferred_element_type=jnp.float32,
    )
    scale = 1.0 / jnp.sqrt(jnp.float32(refs_ref.shape[1]))
    out_ref[...] = (product * scale).astype(jnp.bfloat16)


def score(position, masks, cand, refs):
    total, nbins = cand.shape
    count = refs.shape[0]
    return pl.pallas_call(
        functools.partial(score_kernel, masks),
        out_shape=jax.ShapeDtypeStruct((total, count), jnp.bfloat16),
        grid=(count // REF_ROWS,),
        in_specs=[
            pl.BlockSpec(memory_space=pltpu.SMEM),
            pl.BlockSpec((total, nbins), lambda i: (0, 0)),
            pl.BlockSpec((REF_ROWS, nbins), lambda i: (i, 0)),
        ],
        out_specs=pl.BlockSpec((total, REF_ROWS), lambda i: (0, i)),
        scratch_shapes=[pltpu.VMEM((total, nbins), jnp.bfloat16)],
        name="scores",
    )(position, cand, refs)


def per_device(ndb, ncand, coords, species, miller, offsets, form_amps, form_decay, ref_patterns):
    nbins = ref_patterns.shape[1]
    cand = candidate_patterns(coords, species, miller, offsets, form_amps, form_decay, nbins)
    members = ndb * ncand
    position = (lax.axis_index("db") * ncand + lax.axis_index("cand"))[None].astype(jnp.int32)
    masks = [ncand << bit for bit in range(ndb.bit_length() - 1)]
    masks += [1 << bit for bit in range(ncand.bit_length() - 1)]
    for mask in masks:
        pairs = [(i, i ^ mask) for i in range(members)]
        other = lax.ppermute(cand, ("db", "cand"), pairs)
        cand = jnp.concatenate([cand, other], axis=0)
    refs = standardize_refs(ref_patterns)
    return score(position, tuple(masks), cand, refs)


def solution(mesh):
    in_specs = (
        P(None, ("groups", "db", "cand"), None),
        P(("groups", "db", "cand"), None),
        P(),
        P(),
        P(),
        P(),
        P(("db", "cand"), None),
    )
    out_specs = P("groups", ("db", "cand"))
    body = functools.partial(per_device, mesh.shape["db"], mesh.shape["cand"])
    return jax.shard_map(
        body, mesh=mesh, in_specs=in_specs, out_specs=out_specs, check_vma=False
    )
```

```python
import functools

import jax
import jax.numpy as jnp
from jax import lax
from jax.experimental import pallas as pl
from jax.experimental.pallas import tpu as pltpu
from jax.sharding import PartitionSpec as P

EPSILON = 1e-06
Q_SCALE = 0.0025
PEAK_WIDTH = 0.5
LANES = 128
NORMS = 256
CHUNK = 512
TILE = 128
STAT_ROWS = 1024
SCORE_ROWS = 512
VMEM_LIMIT = 24 << 20

SIN_COEFS = (3.14158208, -5.1671442, 2.54190894, -0.55465711)
COS_COEFS = (0.99999995, -4.93479286, 4.05841191, -1.33188016, 0.21969679)


def horner(coefs, x):
    result = coefs[-1] * x + coefs[-2]
    for coef in coefs[-3::-1]:
        result = result * x + coef
    return result


def flat_lanes(rows):
    return jnp.concatenate([rows[c : c + 1] for c in range(rows.shape[0])], axis=1)


def candidate_kernel(
    coords_hbm, species_hbm, miller_hbm, offsets_hbm, amps_hbm, decay_hbm, refs_hbm,
    out_ref, refs_ref,
    coords_ref, species_ref, miller_ref, offsets_ref, amps_ref, decay_ref,
    places_ref, table_ref, spread_ref, sems,
):
    sources = (coords_hbm, species_hbm, miller_hbm, offsets_hbm, amps_hbm, decay_hbm, refs_hbm)
    targets = (coords_ref, species_ref, miller_ref, offsets_ref, amps_ref, decay_ref, refs_ref)
    copies = [
        pltpu.make_async_copy(source, target, sems.at[i])
        for i, (source, target) in enumerate(zip(sources, targets))
    ]
    for copy in copies:
        copy.start()
    for copy in copies[:-1]:
        copy.wait()
    f32, bf16 = jnp.float32, jnp.bfloat16
    count, atoms = species_ref.shape
    kinds = amps_ref.shape[1]
    reflections = miller_ref.shape[1]
    nbins = out_ref.shape[1]
    nblocks = nbins // LANES
    flat = count * atoms

    pieces = []
    for axis in range(3):
        value = flat_lanes(coords_ref[axis])
        for _ in range(3):
            piece = value.astype(bf16)
            value = value - piece.astype(f32)
            pieces.append(piece.astype(f32))
    places_ref[...] = jnp.concatenate(pieces, axis=0).astype(bf16).T

    norms = lax.broadcasted_iota(jnp.int32, (NORMS, kinds), 0).astype(f32) * Q_SCALE
    table = jnp.zeros((NORMS, kinds), f32)
    for term in range(amps_ref.shape[0]):
        table = table + amps_ref[term : term + 1, :] * jnp.exp(
            -decay_ref[term : term + 1, :] * norms
        )
    onehot = (
        lax.broadcasted_iota(jnp.int32, (kinds, flat), 0) == flat_lanes(species_ref[...])
    ).astype(f32).astype(bf16)
    table_ref[...] = jnp.dot(
        table.astype(bf16), onehot, preferred_element_type=f32
    ).astype(bf16).T

    spread_ref[...] = jnp.zeros_like(spread_ref)

    def step(index, carry):
        cols = pl.ds(pl.multiple_of(index * CHUNK, CHUNK), CHUNK)
        miller = miller_ref[:, cols]
        norm = jnp.sum(miller * miller, axis=0, keepdims=True)
        hkl = miller.astype(f32)
        hkl9 = jnp.concatenate(
            [hkl[axis : axis + 1] for axis in range(3) for _ in range(3)], axis=0
        ).astype(bf16)
        turns = jnp.dot(places_ref[...], hkl9, preferred_element_type=f32)
        pick = (
            lax.broadcasted_iota(jnp.int32, (NORMS, CHUNK), 0) == norm
        ).astype(f32).astype(bf16)
        weight = jnp.dot(table_ref[...], pick, preferred_element_type=f32)
        rows = []
        for c in range(count):
            tiles = []
            for lane in range(0, CHUNK, TILE):
                at = (slice(c * atoms, (c + 1) * atoms), slice(lane, lane + TILE))
                t = turns[at]
                w = weight[at]
                u = t - jnp.round(t)
                square = u * u
                half_sin = u * horner(SIN_COEFS, square)
                half_cos = horner(COS_COEFS, square)
                part = w * half_sin
                real = jnp.sum(w - 2.0 * (part * half_sin), axis=0, keepdims=True)
                imag = 2.0 * jnp.sum(part * half_cos, axis=0, keepdims=True)
                tiles.append(real * real + imag * imag)
            rows.append(jnp.concatenate(tiles, axis=1))
        intensity = jnp.concatenate(rows, axis=0).astype(bf16).astype(f32)
        offset = offsets_ref[:, cols]
        block = offset // LANES
        routed = jnp.concatenate(
            [jnp.where(block == i, intensity, 0.0) for i in range(nblocks)], axis=0
        ).astype(bf16)
        local = (
            lax.broadcasted_iota(jnp.int32, (LANES, CHUNK), 0) == offset - block * LANES
        ).astype(f32).astype(bf16)
        spread_ref[...] += lax.dot_general(
            local, routed, (((1,), (1,)), ((), ())), preferred_element_type=f32
        )
        return carry

    lax.fori_loop(0, reflections // CHUNK, step, 0, unroll=True)

    sums = spread_ref[...].T
    pieces = []
    for _ in range(3):
        piece = sums.astype(bf16)
        sums = sums - piece.astype(f32)
        pieces.append(piece.astype(f32))
    centre = lax.broadcasted_iota(jnp.int32, (LANES, 2 * LANES), 0)
    bins = lax.broadcasted_iota(jnp.int32, (LANES, 2 * LANES), 1)
    bins = jnp.where(bins < LANES + LANES // 2, bins, bins - 2 * LANES)
    distance = (bins - centre).astype(f32) * (1.0 / PEAK_WIDTH)
    profile = jnp.exp(-0.5 * distance * distance).astype(bf16)
    peaks = jnp.dot(
        jnp.concatenate(pieces, axis=0).astype(bf16), profile, preferred_element_type=f32
    )
    rows = count * nblocks
    peaks = peaks[:rows] + peaks[rows : 2 * rows] + peaks[2 * rows :]
    lane = lax.broadcasted_iota(jnp.int32, (count, LANES), 1)
    blocks = []
    for i in range(nblocks):
        own = peaks[i * count : (i + 1) * count, :LANES]
        before = after = jnp.zeros_like(own)
        if i > 0:
            before = peaks[(i - 1) * count : i * count, LANES:]
        if i + 1 < nblocks:
            after = peaks[(i + 1) * count : (i + 2) * count, LANES:]
        blocks.append(own + jnp.where(lane < LANES // 2, before, after))
    pattern = jnp.concatenate(blocks, axis=1)
    centered = pattern - jnp.mean(pattern, axis=1, keepdims=True)
    variance = jnp.mean(centered * centered, axis=1, keepdims=True)
    out_ref[...] = (centered / jnp.sqrt(variance + EPSILON)).astype(bf16)
    copies[-1].wait()


def candidate_patterns(coords, species, miller, offsets, form_amps, form_decay, refs):
    count, atoms = species.shape
    nbins = refs.shape[1]
    args = (coords, species, miller, offsets[None, :], form_amps.T, form_decay.T)
    args = [pltpu.with_memory_space_constraint(arg, pltpu.HBM) for arg in args + (refs,)]
    return pl.pallas_call(
        candidate_kernel,
        out_shape=[
            pltpu.VMEM((count, nbins), jnp.bfloat16),
            pltpu.VMEM(refs.shape, refs.dtype),
        ],
        in_specs=[pl.BlockSpec(memory_space=pltpu.HBM)] * len(args),
        scratch_shapes=[pltpu.VMEM(arg.shape, arg.dtype) for arg in args[:-1]]
        + [
            pltpu.VMEM((count * atoms, 9), jnp.bfloat16),
            pltpu.VMEM((count * atoms, NORMS), jnp.bfloat16),
            pltpu.VMEM((LANES, count * (nbins // LANES)), jnp.float32),
            pltpu.SemaphoreType.DMA((len(args),)),
        ],
        compiler_params=pltpu.CompilerParams(vmem_limit_bytes=VMEM_LIMIT),
        name="candidates",
    )(*args)


VMEM_WHOLE = pl.BlockSpec(memory_space=pltpu.VMEM)


def statistics_kernel(first, refs_ref, after_ref, mean_ref, scale_ref, same_ref):
    f32 = jnp.float32
    nbins = refs_ref.shape[1]
    rows = mean_ref.shape[0]
    ones = jnp.ones((nbins, LANES), jnp.bfloat16)
    block = refs_ref[first : first + rows, :]
    mean = jnp.dot(block, ones, preferred_element_type=f32) * (1.0 / nbins)
    total = jnp.zeros((rows, LANES), f32)
    for lane in range(0, nbins, LANES):
        centered = block[:, lane : lane + LANES].astype(f32) - mean
        total = total + centered * centered
    variance = jnp.sum(total, axis=1, keepdims=True) * (1.0 / nbins)
    mean_ref[...] = mean[:, :1]
    scale_ref[...] = lax.rsqrt(variance + EPSILON) * (1.0 / nbins**0.5)


def statistics(refs, first, rows, after):
    nbins = refs.shape[1]
    return pl.pallas_call(
        functools.partial(statistics_kernel, first),
        out_shape=[pltpu.VMEM((rows, 1), jnp.float32)] * 2 + [pltpu.VMEM(refs.shape, refs.dtype)],
        in_specs=[VMEM_WHOLE, pl.BlockSpec(memory_space=pl.ANY)],
        out_specs=[VMEM_WHOLE] * 3,
        input_output_aliases={0: 2},
        compiler_params=pltpu.CompilerParams(vmem_limit_bytes=VMEM_LIMIT),
        cost_estimate=pl.CostEstimate(
            flops=2 * rows * nbins * LANES, bytes_accessed=2 * rows * nbins, transcendentals=rows
        ),
        name="statistics",
    )(pltpu.with_memory_space_constraint(refs, pltpu.VMEM), after)


def score_kernel(ncand, masks, npieces, *rest):
    cand_refs, (refs_ref, *rest) = rest[: len(masks) + 1], rest[len(masks) + 1 :]
    mean_refs, scale_refs = rest[:npieces], rest[npieces : 2 * npieces]
    out_ref, cand_t_ref = rest[2 * npieces :]
    f32, bf16 = jnp.float32, jnp.bfloat16
    cand = jnp.concatenate([ref[...] for ref in cand_refs], axis=0)
    total, nbins = cand.shape
    block = cand_refs[0].shape[0]
    place = lax.broadcasted_iota(jnp.int32, (total, total), 0)
    group = place // block
    position = lax.axis_index("db") * ncand + lax.axis_index("cand")
    source = jnp.full_like(group, position)
    for bit, mask in enumerate(masks):
        source = source ^ jnp.where((group >> bit) % 2 == 1, mask, 0)
    row = lax.broadcasted_iota(jnp.int32, (total, total), 1)
    order = (row == source * block + place % block).astype(f32).astype(bf16)
    cand_t_ref[...] = lax.dot_general(
        cand, order, (((0,), (0,)), ((), ())), preferred_element_type=f32
    ).astype(bf16)
    sums = jnp.dot(jnp.ones((8, nbins), bf16), cand_t_ref[...], preferred_element_type=f32)[:1]
    rows = mean_refs[0].shape[0]
    for i in range(refs_ref.shape[0] // SCORE_ROWS):
        start = i * SCORE_ROWS
        piece, at = start // rows, slice(start % rows, start % rows + SCORE_ROWS)
        product = jnp.dot(
            refs_ref[start : start + SCORE_ROWS, :], cand_t_ref[...], preferred_element_type=f32
        )
        product = (product - mean_refs[piece][at, :] * sums) * scale_refs[piece][at, :]
        out_ref[:, start : start + SCORE_ROWS] = product.T.astype(bf16)


def score(ncand, masks, cands, refs, means, scales):
    total = sum(cand.shape[0] for cand in cands)
    count, nbins = refs.shape
    return pl.pallas_call(
        functools.partial(score_kernel, ncand, masks, len(means)),
        out_shape=jax.ShapeDtypeStruct((total, count), jnp.bfloat16),
        in_specs=[VMEM_WHOLE] * (len(cands) + 1 + 2 * len(means)),
        scratch_shapes=[pltpu.VMEM((nbins, total), jnp.bfloat16)],
        compiler_params=pltpu.CompilerParams(vmem_limit_bytes=VMEM_LIMIT),
        name="scores",
    )(*cands, pltpu.with_memory_space_constraint(refs, pltpu.VMEM), *means, *scales)


def per_device(ndb, ncand, coords, species, miller, offsets, form_amps, form_decay, ref_patterns):
    count, nbins = ref_patterns.shape
    held, refs = candidate_patterns(
        coords, species, miller, offsets, form_amps, form_decay, ref_patterns
    )
    members = ndb * ncand
    masks = [ncand << bit for bit in range(ndb.bit_length() - 1)]
    masks += [1 << bit for bit in range(ncand.bit_length() - 1)]
    cands, means, scales = [held], [], []
    for stage, mask in enumerate(masks):
        pairs = [(i, i ^ mask) for i in range(members)]
        other = lax.ppermute(held, ("db", "cand"), pairs)
        first = len(means) * STAT_ROWS
        if first < count:
            mean, scale, refs = statistics(refs, first, STAT_ROWS, held)
            means.append(mean)
            scales.append(scale)
            other, mean = lax.optimization_barrier((other, mean))
        cands.append(other)
        held = jnp.concatenate([held, other], axis=0)
    for first in range(len(means) * STAT_ROWS, count, STAT_ROWS):
        mean, scale, refs = statistics(refs, first, STAT_ROWS, held)
        means.append(mean)
        scales.append(scale)
    return score(ncand, tuple(masks), cands, refs, means, scales)


def solution(mesh):
    in_specs = (
        P(None, ("groups", "db", "cand"), None),
        P(("groups", "db", "cand"), None),
        P(),
        P(),
        P(),
        P(),
        P(("db", "cand"), None),
    )
    out_specs = P("groups", ("db", "cand"))
    body = functools.partial(per_device, mesh.shape["db"], mesh.shape["cand"])
    return jax.shard_map(
        body, mesh=mesh, in_specs=in_specs, out_specs=out_specs, check_vma=False
    )
```

```python
import functools

import jax
import jax.numpy as jnp
from jax import lax
from jax.experimental import pallas as pl
from jax.experimental.pallas import tpu as pltpu
from jax.sharding import PartitionSpec as P

EPSILON = 1e-06
Q_SCALE = 0.0025
PEAK_WIDTH = 0.5
LANES = 128
NORMS = 256
CHUNK = 512
TILE = 128
SCORE_ROWS = 512
STAT_UNIT = 256
VMEM_LIMIT = 24 << 20

SIN_COEFS = (3.14158208, -5.1671442, 2.54190894, -0.55465711)
COS_COEFS = (0.99999995, -4.93479286, 4.05841191, -1.33188016, 0.21969679)


def horner(coefs, x):
    result = coefs[-1] * x + coefs[-2]
    for coef in coefs[-3::-1]:
        result = result * x + coef
    return result


def flat_lanes(rows):
    return jnp.concatenate([rows[c : c + 1] for c in range(rows.shape[0])], axis=1)


def candidate_kernel(
    coords_hbm, species_hbm, miller_hbm, offsets_hbm, amps_hbm, decay_hbm, refs_hbm,
    out_ref, refs_ref,
    coords_ref, species_ref, miller_ref, offsets_ref, amps_ref, decay_ref,
    places_ref, table_ref, spread_ref, sems,
):
    sources = (coords_hbm, species_hbm, miller_hbm, offsets_hbm, amps_hbm, decay_hbm, refs_hbm)
    targets = (coords_ref, species_ref, miller_ref, offsets_ref, amps_ref, decay_ref, refs_ref)
    copies = [
        pltpu.make_async_copy(source, target, sems.at[i])
        for i, (source, target) in enumerate(zip(sources, targets))
    ]
    for copy in copies:
        copy.start()
    for copy in copies[:-1]:
        copy.wait()
    f32, bf16 = jnp.float32, jnp.bfloat16
    count, atoms = species_ref.shape
    kinds = amps_ref.shape[1]
    reflections = miller_ref.shape[1]
    nbins = out_ref.shape[1]
    nblocks = nbins // LANES
    flat = count * atoms

    pieces = []
    for axis in range(3):
        value = flat_lanes(coords_ref[axis])
        for _ in range(3):
            piece = value.astype(bf16)
            value = value - piece.astype(f32)
            pieces.append(piece.astype(f32))
    places_ref[...] = jnp.concatenate(pieces, axis=0).astype(bf16).T

    norms = lax.broadcasted_iota(jnp.int32, (NORMS, kinds), 0).astype(f32) * Q_SCALE
    table = jnp.zeros((NORMS, kinds), f32)
    for term in range(amps_ref.shape[0]):
        table = table + amps_ref[term : term + 1, :] * jnp.exp(
            -decay_ref[term : term + 1, :] * norms
        )
    onehot = (
        lax.broadcasted_iota(jnp.int32, (kinds, flat), 0) == flat_lanes(species_ref[...])
    ).astype(f32).astype(bf16)
    table_ref[...] = jnp.dot(
        table.astype(bf16), onehot, preferred_element_type=f32
    ).astype(bf16).T

    spread_ref[...] = jnp.zeros_like(spread_ref)

    def step(index, carry):
        cols = pl.ds(pl.multiple_of(index * CHUNK, CHUNK), CHUNK)
        miller = miller_ref[:, cols]
        norm = jnp.sum(miller * miller, axis=0, keepdims=True)
        hkl = miller.astype(f32)
        hkl9 = jnp.concatenate(
            [hkl[axis : axis + 1] for axis in range(3) for _ in range(3)], axis=0
        ).astype(bf16)
        turns = jnp.dot(places_ref[...], hkl9, preferred_element_type=f32)
        pick = (
            lax.broadcasted_iota(jnp.int32, (NORMS, CHUNK), 0) == norm
        ).astype(f32).astype(bf16)
        weight = jnp.dot(table_ref[...], pick, preferred_element_type=f32)
        rows = []
        for c in range(count):
            tiles = []
            for lane in range(0, CHUNK, TILE):
                at = (slice(c * atoms, (c + 1) * atoms), slice(lane, lane + TILE))
                t = turns[at]
                w = weight[at]
                u = t - jnp.round(t)
                square = u * u
                half_sin = u * horner(SIN_COEFS, square)
                half_cos = horner(COS_COEFS, square)
                part = w * half_sin
                real = jnp.sum(w - 2.0 * (part * half_sin), axis=0, keepdims=True)
                imag = 2.0 * jnp.sum(part * half_cos, axis=0, keepdims=True)
                tiles.append(real * real + imag * imag)
            rows.append(jnp.concatenate(tiles, axis=1))
        intensity = jnp.concatenate(rows, axis=0).astype(bf16).astype(f32)
        offset = offsets_ref[:, cols]
        block = offset // LANES
        routed = jnp.concatenate(
            [jnp.where(block == i, intensity, 0.0) for i in range(nblocks)], axis=0
        ).astype(bf16)
        local = (
            lax.broadcasted_iota(jnp.int32, (LANES, CHUNK), 0) == offset - block * LANES
        ).astype(f32).astype(bf16)
        spread_ref[...] += lax.dot_general(
            local, routed, (((1,), (1,)), ((), ())), preferred_element_type=f32
        )
        return carry

    lax.fori_loop(0, reflections // CHUNK, step, 0, unroll=True)

    sums = spread_ref[...].T
    pieces = []
    for _ in range(3):
        piece = sums.astype(bf16)
        sums = sums - piece.astype(f32)
        pieces.append(piece.astype(f32))
    centre = lax.broadcasted_iota(jnp.int32, (LANES, 2 * LANES), 0)
    bins = lax.broadcasted_iota(jnp.int32, (LANES, 2 * LANES), 1)
    bins = jnp.where(bins < LANES + LANES // 2, bins, bins - 2 * LANES)
    distance = (bins - centre).astype(f32) * (1.0 / PEAK_WIDTH)
    profile = jnp.exp(-0.5 * distance * distance).astype(bf16)
    peaks = jnp.dot(
        jnp.concatenate(pieces, axis=0).astype(bf16), profile, preferred_element_type=f32
    )
    rows = count * nblocks
    peaks = peaks[:rows] + peaks[rows : 2 * rows] + peaks[2 * rows :]
    lane = lax.broadcasted_iota(jnp.int32, (count, LANES), 1)
    blocks = []
    for i in range(nblocks):
        own = peaks[i * count : (i + 1) * count, :LANES]
        before = after = jnp.zeros_like(own)
        if i > 0:
            before = peaks[(i - 1) * count : i * count, LANES:]
        if i + 1 < nblocks:
            after = peaks[(i + 1) * count : (i + 2) * count, LANES:]
        blocks.append(own + jnp.where(lane < LANES // 2, before, after))
    pattern = jnp.concatenate(blocks, axis=1)
    centered = pattern - jnp.mean(pattern, axis=1, keepdims=True)
    variance = jnp.mean(centered * centered, axis=1, keepdims=True)
    out_ref[...] = (centered / jnp.sqrt(variance + EPSILON)).astype(bf16)
    copies[-1].wait()


def candidate_patterns(coords, species, miller, offsets, form_amps, form_decay, refs):
    count, atoms = species.shape
    nbins = refs.shape[1]
    args = (coords, species, miller, offsets[None, :], form_amps.T, form_decay.T)
    args = [pltpu.with_memory_space_constraint(arg, pltpu.HBM) for arg in args + (refs,)]
    return pl.pallas_call(
        candidate_kernel,
        out_shape=[
            pltpu.VMEM((count, nbins), jnp.bfloat16),
            pltpu.VMEM(refs.shape, refs.dtype),
        ],
        in_specs=[pl.BlockSpec(memory_space=pltpu.HBM)] * len(args),
        scratch_shapes=[pltpu.VMEM(arg.shape, arg.dtype) for arg in args[:-1]]
        + [
            pltpu.VMEM((count * atoms, 9), jnp.bfloat16),
            pltpu.VMEM((count * atoms, NORMS), jnp.bfloat16),
            pltpu.VMEM((LANES, count * (nbins // LANES)), jnp.float32),
            pltpu.SemaphoreType.DMA((len(args),)),
        ],
        compiler_params=pltpu.CompilerParams(vmem_limit_bytes=VMEM_LIMIT),
        name="candidates",
    )(*args)


VMEM_WHOLE = pl.BlockSpec(memory_space=pltpu.VMEM)


def statistics_kernel(first, refs_ref, after_ref, mean_ref, scale_ref, same_ref):
    f32 = jnp.float32
    nbins = refs_ref.shape[1]
    rows = mean_ref.shape[0]
    ones = jnp.ones((nbins, LANES), jnp.bfloat16)
    block = refs_ref[first : first + rows, :]
    mean = jnp.dot(block, ones, preferred_element_type=f32) * (1.0 / nbins)
    total = jnp.zeros((rows, LANES), f32)
    for lane in range(0, nbins, LANES):
        centered = block[:, lane : lane + LANES].astype(f32) - mean
        total = total + centered * centered
    variance = jnp.sum(total, axis=1, keepdims=True) * (1.0 / nbins)
    mean_ref[...] = mean[:, :1]
    scale_ref[...] = lax.rsqrt(variance + EPSILON) * (1.0 / nbins**0.5)


def statistics(refs, first, rows, after):
    nbins = refs.shape[1]
    return pl.pallas_call(
        functools.partial(statistics_kernel, first),
        out_shape=[pltpu.VMEM((rows, 1), jnp.float32)] * 2 + [pltpu.VMEM(refs.shape, refs.dtype)],
        in_specs=[VMEM_WHOLE, pl.BlockSpec(memory_space=pl.ANY)],
        out_specs=[VMEM_WHOLE] * 3,
        input_output_aliases={0: 2},
        compiler_params=pltpu.CompilerParams(vmem_limit_bytes=VMEM_LIMIT),
        cost_estimate=pl.CostEstimate(
            flops=2 * rows * nbins * LANES, bytes_accessed=2 * rows * nbins, transcendentals=rows
        ),
        name="statistics",
    )(pltpu.with_memory_space_constraint(refs, pltpu.VMEM), after)


def score_kernel(ncand, masks, npieces, *rest):
    cand_refs, (refs_ref, *rest) = rest[: len(masks) + 1], rest[len(masks) + 1 :]
    mean_refs, scale_refs = rest[:npieces], rest[npieces : 2 * npieces]
    out_ref, cand_t_ref = rest[2 * npieces :]
    f32, bf16 = jnp.float32, jnp.bfloat16
    cand = jnp.concatenate([ref[...] for ref in cand_refs], axis=0)
    total, nbins = cand.shape
    block = cand_refs[0].shape[0]
    place = lax.broadcasted_iota(jnp.int32, (total, total), 0)
    group = place // block
    position = lax.axis_index("db") * ncand + lax.axis_index("cand")
    source = jnp.full_like(group, position)
    for bit, mask in enumerate(masks):
        source = source ^ jnp.where((group >> bit) % 2 == 1, mask, 0)
    row = lax.broadcasted_iota(jnp.int32, (total, total), 1)
    order = (row == source * block + place % block).astype(f32).astype(bf16)
    cand_t_ref[...] = lax.dot_general(
        cand, order, (((0,), (0,)), ((), ())), preferred_element_type=f32
    ).astype(bf16)
    sums = jnp.dot(jnp.ones((8, nbins), bf16), cand_t_ref[...], preferred_element_type=f32)[:1]
    means, scales = (
        jnp.concatenate([ref[...] for ref in refs], axis=0) for refs in (mean_refs, scale_refs)
    )
    for start in range(0, refs_ref.shape[0], SCORE_ROWS):
        rows = slice(start, start + SCORE_ROWS)
        product = jnp.dot(refs_ref[rows, :], cand_t_ref[...], preferred_element_type=f32)
        product = (product - means[rows] * sums) * scales[rows]
        out_ref[:, rows] = product.T.astype(bf16)


def score(ncand, masks, cands, refs, means, scales):
    total = sum(cand.shape[0] for cand in cands)
    count, nbins = refs.shape
    return pl.pallas_call(
        functools.partial(score_kernel, ncand, masks, len(means)),
        out_shape=jax.ShapeDtypeStruct((total, count), jnp.bfloat16),
        in_specs=[VMEM_WHOLE] * (len(cands) + 1 + 2 * len(means)),
        scratch_shapes=[pltpu.VMEM((nbins, total), jnp.bfloat16)],
        compiler_params=pltpu.CompilerParams(vmem_limit_bytes=VMEM_LIMIT),
        name="scores",
    )(*cands, pltpu.with_memory_space_constraint(refs, pltpu.VMEM), *means, *scales)


def per_device(ndb, ncand, coords, species, miller, offsets, form_amps, form_decay, ref_patterns):
    count, nbins = ref_patterns.shape
    held, refs = candidate_patterns(
        coords, species, miller, offsets, form_amps, form_decay, ref_patterns
    )
    members = ndb * ncand
    core = ncand
    masks = [core | ncand << bit for bit in range(1, ndb.bit_length() - 1)]
    masks += [core | 1 << bit for bit in range(ncand.bit_length() - 1)]
    masks.append(core)
    share = -(-count * 5 // 16 // STAT_UNIT) * STAT_UNIT
    cands, means, scales = [held], [], []
    first = 0
    for mask in masks:
        other = lax.ppermute(held, ("db", "cand"), [(i, i ^ mask) for i in range(members)])
        rows = min(share, count - first)
        if rows > 0:
            mean, scale, refs = statistics(refs, first, rows, held)
            means.append(mean)
            scales.append(scale)
            first += rows
            other, mean = lax.optimization_barrier((other, mean))
        cands.append(other)
        held = jnp.concatenate([held, other], axis=0)
    if first < count:
        mean, scale, refs = statistics(refs, first, count - first, held)
        means.append(mean)
        scales.append(scale)
    return score(ncand, tuple(masks), cands, refs, means, scales)


def solution(mesh):
    in_specs = (
        P(None, ("groups", "db", "cand"), None),
        P(("groups", "db", "cand"), None),
        P(),
        P(),
        P(),
        P(),
        P(("db", "cand"), None),
    )
    out_specs = P("groups", ("db", "cand"))
    body = functools.partial(per_device, mesh.shape["db"], mesh.shape["cand"])
    return jax.shard_map(
        body, mesh=mesh, in_specs=in_specs, out_specs=out_specs, check_vma=False
    )
```

```python
import functools

import jax
import jax.numpy as jnp
from jax import lax
from jax.experimental import pallas as pl
from jax.experimental.pallas import tpu as pltpu
from jax.sharding import PartitionSpec as P

EPSILON = 1e-06
Q_SCALE = 0.0025
PEAK_WIDTH = 0.5
LANES = 128
SIDE = 9
NORMS = 208
CHUNK = 4096
SCORE_ROWS = 512
STAT_UNIT = 256
VMEM_LIMIT = 24 << 20

SIN_COEFS = (3.14159258, -5.1677069, 2.55003164, -0.59804645, 0.07722225)
COS_COEFS = (0.99999995, -4.93479286, 4.05841191, -1.33188016, 0.21969679)


def horner(coefs, x):
    result = coefs[-1] * x + coefs[-2]
    for coef in coefs[-3::-1]:
        result = result * x + coef
    return result


def flat_lanes(rows):
    return jnp.concatenate([rows[c : c + 1] for c in range(rows.shape[0])], axis=1)


def candidate_kernel(
    coords_hbm, species_hbm, miller_hbm, offsets_hbm, amps_hbm, decay_hbm, refs_hbm,
    out_ref, refs_ref,
    coords_ref, species_ref, miller_ref, offsets_ref, amps_ref, decay_ref,
    grid_ref, spread_ref, sems,
):
    sources = (coords_hbm, species_hbm, miller_hbm, offsets_hbm, amps_hbm, decay_hbm, refs_hbm)
    targets = (coords_ref, species_ref, miller_ref, offsets_ref, amps_ref, decay_ref, refs_ref)
    copies = [
        pltpu.make_async_copy(source, target, sems.at[i])
        for i, (source, target) in enumerate(zip(sources, targets))
    ]
    for copy in copies:
        copy.start()
    for copy in copies[:-1]:
        copy.wait()
    f32, bf16 = jnp.float32, jnp.bfloat16
    count, atoms = species_ref.shape
    kinds = amps_ref.shape[1]
    reflections = miller_ref.shape[1]
    nbins = out_ref.shape[1]
    nblocks = nbins // LANES
    flat = count * atoms

    pieces = []
    for axis in range(3):
        value = flat_lanes(coords_ref[axis])
        for _ in range(3):
            piece = value.astype(bf16)
            value = value - piece.astype(f32)
            pieces.append(piece.astype(f32))
    places = jnp.concatenate(pieces, axis=0).astype(bf16).T

    axis = lax.broadcasted_iota(jnp.int32, (9, 3 * LANES), 0) // 3
    column = lax.broadcasted_iota(jnp.int32, (9, 3 * LANES), 1)
    tile = column // LANES
    point = column - tile * LANES
    index1 = point // SIDE
    index2 = point - index1 * SIDE
    index2 = jnp.where(tile == 0, index2, -index2)
    yz = jnp.where(axis == 1, index1, jnp.where(axis == 2, index2, 0))
    indices = jnp.where(tile == 2, jnp.where(axis == 0, point, 0), yz)
    turns = jnp.dot(places, indices.astype(f32).astype(bf16), preferred_element_type=f32)
    u = turns - jnp.round(turns)
    square = u * u
    half_sin = u * horner(SIN_COEFS, square)
    half_cos = horner(COS_COEFS, square)
    cosine = 1.0 - 2.0 * (half_sin * half_sin)
    sine = 2.0 * (half_sin * half_cos)

    norms = lax.broadcasted_iota(jnp.int32, (NORMS, kinds), 0).astype(f32) * Q_SCALE
    table = jnp.zeros((NORMS, kinds), f32)
    for term in range(amps_ref.shape[0]):
        table = table + amps_ref[term : term + 1, :] * jnp.exp(
            -decay_ref[term : term + 1, :] * norms
        )
    onehot = (
        lax.broadcasted_iota(jnp.int32, (kinds, flat), 0) == flat_lanes(species_ref[...])
    ).astype(f32).astype(bf16)
    atom_table = jnp.dot(
        table.astype(bf16), onehot, preferred_element_type=f32
    ).astype(bf16).T
    point = lax.broadcasted_iota(jnp.int32, (NORMS, LANES), 1)
    index1 = point // SIDE
    index2 = point - index1 * SIDE
    rest = lax.broadcasted_iota(jnp.int32, (NORMS, LANES), 0) - index1 * index1 - index2 * index2
    pick = jnp.concatenate(
        [(rest == h0 * h0).astype(f32).astype(bf16) for h0 in range(SIDE)], axis=1
    )
    weight = jnp.dot(atom_table, pick, preferred_element_type=f32)

    for c in range(count):
        atom = slice(c * atoms, (c + 1) * atoms)
        for h0 in range(SIDE):
            w = weight[atom, h0 * LANES : (h0 + 1) * LANES]
            w_cos = w * cosine[atom, 2 * LANES + h0 : 2 * LANES + h0 + 1]
            w_sin = w * sine[atom, 2 * LANES + h0 : 2 * LANES + h0 + 1]
            for minus in range(2):
                cos12 = cosine[atom, minus * LANES : (minus + 1) * LANES]
                sin12 = sine[atom, minus * LANES : (minus + 1) * LANES]
                cc = jnp.sum(w_cos * cos12, axis=0, keepdims=True)
                ss = jnp.sum(w_sin * sin12, axis=0, keepdims=True)
                cs = jnp.sum(w_cos * sin12, axis=0, keepdims=True)
                sc = jnp.sum(w_sin * cos12, axis=0, keepdims=True)
                row = (minus * SIDE + h0) * count + c
                real, imag = cc - ss, cs + sc
                grid_ref[row : row + 1, :] = real * real + imag * imag
                real, imag = cc + ss, cs - sc
                row = row + 2 * SIDE * count
                grid_ref[row : row + 1, :] = real * real + imag * imag
    grid = grid_ref[...].astype(bf16)
    group = lax.broadcasted_iota(jnp.int32, (4 * SIDE * count, CHUNK), 0) // count

    spread_ref[...] = jnp.zeros_like(spread_ref)

    def step(index, carry):
        cols = pl.ds(pl.multiple_of(index * CHUNK, CHUNK), CHUNK)
        miller = miller_ref[:, cols]
        miller = jnp.where(miller[1:2] < 0, -miller, miller)
        size = jnp.abs(miller)
        signs = jnp.where(miller < 0, 1, 0)
        place = size[1:2] * SIDE + size[2:3]
        chosen = (2 * signs[0:1] + signs[2:3]) * SIDE + size[0:1]
        at_place = (
            lax.broadcasted_iota(jnp.int32, (LANES, CHUNK), 0) == place
        ).astype(f32).astype(bf16)
        values = jnp.dot(grid, at_place, preferred_element_type=f32)
        values = jnp.where(group == chosen, values, 0.0)
        values = jnp.sum(values.reshape(-1, 8, CHUNK), axis=0)
        intensity = jnp.sum(values.reshape(8 // count, count, CHUNK), axis=0)

        offset = offsets_ref[:, cols]
        block = offset // LANES
        routed = jnp.concatenate(
            [jnp.where(block == i, intensity, 0.0) for i in range(nblocks)], axis=0
        ).astype(bf16)
        local = (
            lax.broadcasted_iota(jnp.int32, (LANES, CHUNK), 0) == offset - block * LANES
        ).astype(f32).astype(bf16)
        spread_ref[...] += lax.dot_general(
            local, routed, (((1,), (1,)), ((), ())), preferred_element_type=f32
        )
        return carry

    lax.fori_loop(0, reflections // CHUNK, step, 0, unroll=True)

    sums = spread_ref[...].T
    pieces = []
    for _ in range(3):
        piece = sums.astype(bf16)
        sums = sums - piece.astype(f32)
        pieces.append(piece.astype(f32))
    centre = lax.broadcasted_iota(jnp.int32, (LANES, 2 * LANES), 0)
    bins = lax.broadcasted_iota(jnp.int32, (LANES, 2 * LANES), 1)
    bins = jnp.where(bins < LANES + LANES // 2, bins, bins - 2 * LANES)
    distance = (bins - centre).astype(f32) * (1.0 / PEAK_WIDTH)
    profile = jnp.exp(-0.5 * distance * distance).astype(bf16)
    peaks = jnp.dot(
        jnp.concatenate(pieces, axis=0).astype(bf16), profile, preferred_element_type=f32
    )
    rows = count * nblocks
    peaks = peaks[:rows] + peaks[rows : 2 * rows] + peaks[2 * rows :]
    lane = lax.broadcasted_iota(jnp.int32, (count, LANES), 1)
    blocks = []
    for i in range(nblocks):
        own = peaks[i * count : (i + 1) * count, :LANES]
        before = after = jnp.zeros_like(own)
        if i > 0:
            before = peaks[(i - 1) * count : i * count, LANES:]
        if i + 1 < nblocks:
            after = peaks[(i + 1) * count : (i + 2) * count, LANES:]
        blocks.append(own + jnp.where(lane < LANES // 2, before, after))
    pattern = jnp.concatenate(blocks, axis=1)
    centered = pattern - jnp.mean(pattern, axis=1, keepdims=True)
    variance = jnp.mean(centered * centered, axis=1, keepdims=True)
    out_ref[...] = (centered / jnp.sqrt(variance + EPSILON)).astype(bf16)
    copies[-1].wait()


def candidate_patterns(coords, species, miller, offsets, form_amps, form_decay, refs):
    count, atoms = species.shape
    nbins = refs.shape[1]
    args = (coords, species, miller, offsets[None, :], form_amps.T, form_decay.T)
    args = [pltpu.with_memory_space_constraint(arg, pltpu.HBM) for arg in args + (refs,)]
    return pl.pallas_call(
        candidate_kernel,
        out_shape=[
            pltpu.VMEM((count, nbins), jnp.bfloat16),
            pltpu.VMEM(refs.shape, refs.dtype),
        ],
        in_specs=[pl.BlockSpec(memory_space=pltpu.HBM)] * len(args),
        scratch_shapes=[pltpu.VMEM(arg.shape, arg.dtype) for arg in args[:-1]]
        + [
            pltpu.VMEM((4 * SIDE * count, LANES), jnp.float32),
            pltpu.VMEM((LANES, count * (nbins // LANES)), jnp.float32),
            pltpu.SemaphoreType.DMA((len(args),)),
        ],
        compiler_params=pltpu.CompilerParams(vmem_limit_bytes=VMEM_LIMIT),
        name="candidates",
    )(*args)


VMEM_WHOLE = pl.BlockSpec(memory_space=pltpu.VMEM)


def statistics_kernel(first, refs_ref, after_ref, mean_ref, scale_ref, same_ref):
    f32 = jnp.float32
    nbins = refs_ref.shape[1]
    rows = mean_ref.shape[0]
    ones = jnp.ones((nbins, LANES), jnp.bfloat16)
    block = refs_ref[first : first + rows, :]
    mean = jnp.dot(block, ones, preferred_element_type=f32) * (1.0 / nbins)
    total = jnp.zeros((rows, LANES), f32)
    for lane in range(0, nbins, LANES):
        centered = block[:, lane : lane + LANES].astype(f32) - mean
        total = total + centered * centered
    variance = jnp.sum(total, axis=1, keepdims=True) * (1.0 / nbins)
    mean_ref[...] = mean[:, :1]
    scale_ref[...] = lax.rsqrt(variance + EPSILON) * (1.0 / nbins**0.5)


def statistics(refs, first, rows, after):
    nbins = refs.shape[1]
    return pl.pallas_call(
        functools.partial(statistics_kernel, first),
        out_shape=[pltpu.VMEM((rows, 1), jnp.float32)] * 2 + [pltpu.VMEM(refs.shape, refs.dtype)],
        in_specs=[VMEM_WHOLE, pl.BlockSpec(memory_space=pl.ANY)],
        out_specs=[VMEM_WHOLE] * 3,
        input_output_aliases={0: 2},
        compiler_params=pltpu.CompilerParams(vmem_limit_bytes=VMEM_LIMIT),
        cost_estimate=pl.CostEstimate(
            flops=2 * rows * nbins * LANES, bytes_accessed=2 * rows * nbins, transcendentals=rows
        ),
        name="statistics",
    )(pltpu.with_memory_space_constraint(refs, pltpu.VMEM), after)


def score_kernel(ncand, masks, npieces, *rest):
    cand_refs, (refs_ref, *rest) = rest[: len(masks) + 1], rest[len(masks) + 1 :]
    mean_refs, scale_refs = rest[:npieces], rest[npieces : 2 * npieces]
    out_ref, cand_t_ref = rest[2 * npieces :]
    f32, bf16 = jnp.float32, jnp.bfloat16
    cand = jnp.concatenate([ref[...] for ref in cand_refs], axis=0)
    total, nbins = cand.shape
    block = cand_refs[0].shape[0]
    place = lax.broadcasted_iota(jnp.int32, (total, total), 0)
    group = place // block
    position = lax.axis_index("db") * ncand + lax.axis_index("cand")
    source = jnp.full_like(group, position)
    for bit, mask in enumerate(masks):
        source = source ^ jnp.where((group >> bit) % 2 == 1, mask, 0)
    row = lax.broadcasted_iota(jnp.int32, (total, total), 1)
    order = (row == source * block + place % block).astype(f32).astype(bf16)
    cand_t_ref[...] = lax.dot_general(
        cand, order, (((0,), (0,)), ((), ())), preferred_element_type=f32
    ).astype(bf16)
    sums = jnp.dot(jnp.ones((8, nbins), bf16), cand_t_ref[...], preferred_element_type=f32)[:1]
    means, scales = (
        jnp.concatenate([ref[...] for ref in refs], axis=0) for refs in (mean_refs, scale_refs)
    )
    for start in range(0, refs_ref.shape[0], SCORE_ROWS):
        rows = slice(start, start + SCORE_ROWS)
        product = jnp.dot(refs_ref[rows, :], cand_t_ref[...], preferred_element_type=f32)
        product = (product - means[rows] * sums) * scales[rows]
        out_ref[:, rows] = product.T.astype(bf16)


def score(ncand, masks, cands, refs, means, scales):
    total = sum(cand.shape[0] for cand in cands)
    count, nbins = refs.shape
    return pl.pallas_call(
        functools.partial(score_kernel, ncand, masks, len(means)),
        out_shape=jax.ShapeDtypeStruct((total, count), jnp.bfloat16),
        in_specs=[VMEM_WHOLE] * (len(cands) + 1 + 2 * len(means)),
        scratch_shapes=[pltpu.VMEM((nbins, total), jnp.bfloat16)],
        compiler_params=pltpu.CompilerParams(vmem_limit_bytes=VMEM_LIMIT),
        name="scores",
    )(*cands, pltpu.with_memory_space_constraint(refs, pltpu.VMEM), *means, *scales)


def per_device(ndb, ncand, coords, species, miller, offsets, form_amps, form_decay, ref_patterns):
    count, nbins = ref_patterns.shape
    held, refs = candidate_patterns(
        coords, species, miller, offsets, form_amps, form_decay, ref_patterns
    )
    members = ndb * ncand
    core = ncand
    masks = [core | ncand << bit for bit in range(1, ndb.bit_length() - 1)]
    masks += [core | 1 << bit for bit in range(ncand.bit_length() - 1)]
    masks.append(core)
    share = -(-count * 5 // 16 // STAT_UNIT) * STAT_UNIT
    cands, means, scales = [held], [], []
    first = 0
    for mask in masks:
        other = lax.ppermute(held, ("db", "cand"), [(i, i ^ mask) for i in range(members)])
        rows = min(share, count - first)
        if rows > 0:
            mean, scale, refs = statistics(refs, first, rows, held)
            means.append(mean)
            scales.append(scale)
            first += rows
            other, mean = lax.optimization_barrier((other, mean))
        cands.append(other)
        held = jnp.concatenate([held, other], axis=0)
    if first < count:
        mean, scale, refs = statistics(refs, first, count - first, held)
        means.append(mean)
        scales.append(scale)
    return score(ncand, tuple(masks), cands, refs, means, scales)


def solution(mesh):
    in_specs = (
        P(None, ("groups", "db", "cand"), None),
        P(("groups", "db", "cand"), None),
        P(),
        P(),
        P(),
        P(),
        P(("db", "cand"), None),
    )
    out_specs = P("groups", ("db", "cand"))
    body = functools.partial(per_device, mesh.shape["db"], mesh.shape["cand"])
    return jax.shard_map(
        body, mesh=mesh, in_specs=in_specs, out_specs=out_specs, check_vma=False
    )
```

```python
import functools

import jax
import jax.numpy as jnp
from jax import lax
from jax.experimental import pallas as pl
from jax.experimental.pallas import tpu as pltpu
from jax.sharding import PartitionSpec as P

EPSILON = 1e-06
Q_SCALE = 0.0025
PEAK_WIDTH = 0.5
LANES = 128
SIDE = 9
NORMS = 208
CHUNK = 4096
SCORE_ROWS = 512
STAT_UNIT = 256
STAT_STEP = 256
VMEM_LIMIT = 24 << 20

SIN_COEFS = (3.14159258, -5.1677069, 2.55003164, -0.59804645, 0.07722225)
COS_COEFS = (0.99999995, -4.93479286, 4.05841191, -1.33188016, 0.21969679)


def horner(coefs, x):
    result = coefs[-1] * x + coefs[-2]
    for coef in coefs[-3::-1]:
        result = result * x + coef
    return result


def flat_lanes(rows):
    return jnp.concatenate([rows[c : c + 1] for c in range(rows.shape[0])], axis=1)


def candidate_kernel(
    coords_hbm, species_hbm, miller_hbm, offsets_hbm, amps_hbm, decay_hbm, refs_hbm,
    out_ref, refs_ref,
    coords_ref, species_ref, miller_ref, offsets_ref, amps_ref, decay_ref,
    grid_ref, spread_ref, sems,
):
    sources = (coords_hbm, species_hbm, miller_hbm, offsets_hbm, amps_hbm, decay_hbm, refs_hbm)
    targets = (coords_ref, species_ref, miller_ref, offsets_ref, amps_ref, decay_ref, refs_ref)
    copies = [
        pltpu.make_async_copy(source, target, sems.at[i])
        for i, (source, target) in enumerate(zip(sources, targets))
    ]
    for copy in copies:
        copy.start()
    f32, bf16 = jnp.float32, jnp.bfloat16
    count, atoms = species_ref.shape
    kinds = amps_ref.shape[1]
    reflections = miller_ref.shape[1]
    nbins = out_ref.shape[1]
    nblocks = nbins // LANES
    flat = count * atoms


    axis = lax.broadcasted_iota(jnp.int32, (9, 3 * LANES), 0) // 3
    column = lax.broadcasted_iota(jnp.int32, (9, 3 * LANES), 1)
    tile = column // LANES
    point = column - tile * LANES
    index1 = point // SIDE
    index2 = point - index1 * SIDE
    index2 = jnp.where(tile == 0, index2, -index2)
    yz = jnp.where(axis == 1, index1, jnp.where(axis == 2, index2, 0))
    indices = jnp.where(tile == 2, jnp.where(axis == 0, point, 0), yz)
    indices = indices.astype(f32).astype(bf16)

    point = lax.broadcasted_iota(jnp.int32, (NORMS, LANES), 1)
    index1 = point // SIDE
    index2 = point - index1 * SIDE
    rest = lax.broadcasted_iota(jnp.int32, (NORMS, LANES), 0) - index1 * index1 - index2 * index2
    pick = jnp.concatenate(
        [(rest == h0 * h0).astype(f32).astype(bf16) for h0 in range(SIDE)], axis=1
    )

    centre = lax.broadcasted_iota(jnp.int32, (LANES, 2 * LANES), 0)
    bins = lax.broadcasted_iota(jnp.int32, (LANES, 2 * LANES), 1)
    bins = jnp.where(bins < LANES + LANES // 2, bins, bins - 2 * LANES)
    distance = (bins - centre).astype(f32) * (1.0 / PEAK_WIDTH)
    profile = jnp.exp(-0.5 * distance * distance).astype(bf16)

    for copy in copies[:2] + copies[4:6]:
        copy.wait()
    pieces = []
    for axis in range(3):
        value = flat_lanes(coords_ref[axis])
        for _ in range(3):
            piece = value.astype(bf16)
            value = value - piece.astype(f32)
            pieces.append(piece.astype(f32))
    places = jnp.concatenate(pieces, axis=0).astype(bf16).T

    turns = jnp.dot(places, indices, preferred_element_type=f32)
    u = turns - jnp.round(turns)
    square = u * u
    half_sin = u * horner(SIN_COEFS, square)
    half_cos = horner(COS_COEFS, square)
    cosine = 1.0 - 2.0 * (half_sin * half_sin)
    sine = 2.0 * (half_sin * half_cos)

    norms = lax.broadcasted_iota(jnp.int32, (NORMS, kinds), 0).astype(f32) * Q_SCALE
    table = jnp.zeros((NORMS, kinds), f32)
    for term in range(amps_ref.shape[0]):
        table = table + amps_ref[term : term + 1, :] * jnp.exp(
            -decay_ref[term : term + 1, :] * norms
        )
    onehot = (
        lax.broadcasted_iota(jnp.int32, (kinds, flat), 0) == flat_lanes(species_ref[...])
    ).astype(f32).astype(bf16)
    atom_table = jnp.dot(
        table.astype(bf16), onehot, preferred_element_type=f32
    ).astype(bf16).T
    weight = jnp.dot(atom_table, pick, preferred_element_type=f32)

    points = 2 * SIDE * count
    for c in range(count):
        atom = slice(c * atoms, (c + 1) * atoms)
        for h0 in range(SIDE):
            w = weight[atom, h0 * LANES : (h0 + 1) * LANES]
            w_cos = w * cosine[atom, 2 * LANES + h0 : 2 * LANES + h0 + 1]
            w_sin = w * sine[atom, 2 * LANES + h0 : 2 * LANES + h0 + 1]
            for minus in range(2):
                cos12 = cosine[atom, minus * LANES : (minus + 1) * LANES]
                sin12 = sine[atom, minus * LANES : (minus + 1) * LANES]
                terms = (w_cos * cos12, w_sin * sin12, w_cos * sin12, w_sin * cos12)
                for i, term in enumerate(terms):
                    row = (i * points + (minus * SIDE + h0) * count + c) * 8
                    grid_ref[row : row + 8, :] = jnp.sum(term.reshape(-1, 8, LANES), axis=0)
    cc, ss, cs, sc = (
        sum(grid_ref[pl.ds(i * points * 8 + j, points, stride=8), :] for j in range(8))
        for i in range(4)
    )
    plus = (cc - ss) * (cc - ss) + (cs + sc) * (cs + sc)
    minus = (cc + ss) * (cc + ss) + (cs - sc) * (cs - sc)
    grid = jnp.concatenate([plus, minus], axis=0).astype(bf16)
    group = lax.broadcasted_iota(jnp.int32, (4 * SIDE * count, CHUNK), 0) // count

    for copy in copies[2:4]:
        copy.wait()
    spread_ref[...] = jnp.zeros_like(spread_ref)

    def step(index, carry):
        cols = pl.ds(pl.multiple_of(index * CHUNK, CHUNK), CHUNK)
        miller = miller_ref[:, cols]
        miller = jnp.where(miller[1:2] < 0, -miller, miller)
        size = jnp.abs(miller)
        signs = jnp.where(miller < 0, 1, 0)
        place = size[1:2] * SIDE + size[2:3]
        chosen = (2 * signs[0:1] + signs[2:3]) * SIDE + size[0:1]
        at_place = (
            lax.broadcasted_iota(jnp.int32, (LANES, CHUNK), 0) == place
        ).astype(f32).astype(bf16)
        values = jnp.dot(grid, at_place, preferred_element_type=f32)
        values = jnp.where(group == chosen, values, 0.0)
        values = jnp.sum(values.reshape(-1, 8, CHUNK), axis=0)
        intensity = jnp.sum(values.reshape(8 // count, count, CHUNK), axis=0)

        offset = offsets_ref[:, cols]
        block = offset // LANES
        routed = jnp.concatenate(
            [jnp.where(block == i, intensity, 0.0) for i in range(nblocks)], axis=0
        ).astype(bf16)
        local = (
            lax.broadcasted_iota(jnp.int32, (LANES, CHUNK), 0) == offset - block * LANES
        ).astype(f32).astype(bf16)
        spread_ref[...] += lax.dot_general(
            local, routed, (((1,), (1,)), ((), ())), preferred_element_type=f32
        )
        return carry

    lax.fori_loop(0, reflections // CHUNK, step, 0, unroll=True)

    sums = spread_ref[...].T
    pieces = []
    for _ in range(3):
        piece = sums.astype(bf16)
        sums = sums - piece.astype(f32)
        pieces.append(piece.astype(f32))
    peaks = jnp.dot(
        jnp.concatenate(pieces, axis=0).astype(bf16), profile, preferred_element_type=f32
    )
    rows = count * nblocks
    peaks = peaks[:rows] + peaks[rows : 2 * rows] + peaks[2 * rows :]
    lane = lax.broadcasted_iota(jnp.int32, (count, LANES), 1)
    blocks = []
    for i in range(nblocks):
        own = peaks[i * count : (i + 1) * count, :LANES]
        before = after = jnp.zeros_like(own)
        if i > 0:
            before = peaks[(i - 1) * count : i * count, LANES:]
        if i + 1 < nblocks:
            after = peaks[(i + 1) * count : (i + 2) * count, LANES:]
        blocks.append(own + jnp.where(lane < LANES // 2, before, after))
    pattern = jnp.concatenate(blocks, axis=1)
    centered = pattern - jnp.mean(pattern, axis=1, keepdims=True)
    variance = jnp.mean(centered * centered, axis=1, keepdims=True)
    out_ref[...] = (centered / jnp.sqrt(variance + EPSILON)).astype(bf16)
    copies[-1].wait()


def candidate_patterns(coords, species, miller, offsets, form_amps, form_decay, refs):
    count, atoms = species.shape
    nbins = refs.shape[1]
    args = (coords, species, miller, offsets[None, :], form_amps.T, form_decay.T)
    args = [pltpu.with_memory_space_constraint(arg, pltpu.HBM) for arg in args + (refs,)]
    return pl.pallas_call(
        candidate_kernel,
        out_shape=[
            pltpu.VMEM((count, nbins), jnp.bfloat16),
            pltpu.VMEM(refs.shape, refs.dtype),
        ],
        in_specs=[pl.BlockSpec(memory_space=pltpu.HBM)] * len(args),
        scratch_shapes=[pltpu.VMEM(arg.shape, arg.dtype) for arg in args[:-1]]
        + [
            pltpu.VMEM((8 * 8 * SIDE * count, LANES), jnp.float32),
            pltpu.VMEM((LANES, count * (nbins // LANES)), jnp.float32),
            pltpu.SemaphoreType.DMA((len(args),)),
        ],
        compiler_params=pltpu.CompilerParams(vmem_limit_bytes=VMEM_LIMIT),
        name="candidates",
    )(*args)


VMEM_WHOLE = pl.BlockSpec(memory_space=pltpu.VMEM)


def statistics_kernel(first, refs_ref, after_ref, mean_ref, scale_ref, same_ref):
    f32 = jnp.float32
    nbins = refs_ref.shape[1]
    rows = mean_ref.shape[0]
    for at in range(first, first + rows, STAT_STEP):
        tiles = [
            refs_ref[at : at + STAT_STEP, lane : lane + LANES].astype(f32)
            for lane in range(0, nbins, LANES)
        ]
        mean = jnp.sum(sum(tiles[1:], tiles[0]), axis=1, keepdims=True) * (1.0 / nbins)
        total = jnp.zeros((STAT_STEP, LANES), f32)
        for tile in tiles:
            total = total + (tile - mean) * (tile - mean)
        variance = jnp.sum(total, axis=1, keepdims=True) * (1.0 / nbins)
        mean_ref[at - first : at - first + STAT_STEP, :] = mean
        scale_ref[at - first : at - first + STAT_STEP, :] = lax.rsqrt(variance + EPSILON) * (1.0 / nbins**0.5)


def statistics(refs, first, rows, after):
    nbins = refs.shape[1]
    return pl.pallas_call(
        functools.partial(statistics_kernel, first),
        out_shape=[pltpu.VMEM((rows, 1), jnp.float32)] * 2 + [pltpu.VMEM(refs.shape, refs.dtype)],
        in_specs=[VMEM_WHOLE, pl.BlockSpec(memory_space=pl.ANY)],
        out_specs=[VMEM_WHOLE] * 3,
        input_output_aliases={0: 2},
        compiler_params=pltpu.CompilerParams(vmem_limit_bytes=VMEM_LIMIT),
        cost_estimate=pl.CostEstimate(
            flops=2 * rows * nbins * LANES, bytes_accessed=2 * rows * nbins, transcendentals=rows
        ),
        name="statistics",
    )(pltpu.with_memory_space_constraint(refs, pltpu.VMEM), after)


def score_kernel(ncand, masks, npieces, *rest):
    cand_refs, (refs_ref, *rest) = rest[: len(masks) + 1], rest[len(masks) + 1 :]
    mean_refs, scale_refs = rest[:npieces], rest[npieces : 2 * npieces]
    out_ref, cand_t_ref, held_ref, sems = rest[2 * npieces :]
    f32, bf16 = jnp.float32, jnp.bfloat16
    cand = jnp.concatenate([ref[...] for ref in cand_refs], axis=0)
    total, nbins = cand.shape
    block = cand_refs[0].shape[0]
    place = lax.broadcasted_iota(jnp.int32, (total, total), 0)
    group = place // block
    position = lax.axis_index("db") * ncand + lax.axis_index("cand")
    source = jnp.full_like(group, position)
    for bit, mask in enumerate(masks):
        source = source ^ jnp.where((group >> bit) % 2 == 1, mask, 0)
    row = lax.broadcasted_iota(jnp.int32, (total, total), 1)
    order = (row == source * block + place % block).astype(f32).astype(bf16)
    cand_t_ref[...] = lax.dot_general(
        cand, order, (((0,), (0,)), ((), ())), preferred_element_type=f32
    ).astype(bf16)
    sums = jnp.dot(jnp.ones((8, nbins), bf16), cand_t_ref[...], preferred_element_type=f32)[:1]
    means, scales = (
        jnp.concatenate([ref[...] for ref in refs], axis=0) for refs in (mean_refs, scale_refs)
    )
    copies = []
    for i, start in enumerate(range(0, refs_ref.shape[0], SCORE_ROWS)):
        rows = slice(start, start + SCORE_ROWS)
        product = jnp.dot(refs_ref[rows, :], cand_t_ref[...], preferred_element_type=f32)
        product = (product - means[rows] * sums) * scales[rows]
        held_ref[:, rows] = product.T.astype(bf16)
        copy = pltpu.make_async_copy(held_ref.at[:, rows], out_ref.at[:, rows], sems.at[i])
        copy.start()
        copies.append(copy)
    for copy in copies:
        copy.wait()


def score(ncand, masks, cands, refs, means, scales):
    total = sum(cand.shape[0] for cand in cands)
    count, nbins = refs.shape
    return pl.pallas_call(
        functools.partial(score_kernel, ncand, masks, len(means)),
        out_shape=jax.ShapeDtypeStruct((total, count), jnp.bfloat16),
        in_specs=[VMEM_WHOLE] * (len(cands) + 1 + 2 * len(means)),
        out_specs=pl.BlockSpec(memory_space=pltpu.HBM),
        scratch_shapes=[
            pltpu.VMEM((nbins, total), jnp.bfloat16),
            pltpu.VMEM((total, count), jnp.bfloat16),
            pltpu.SemaphoreType.DMA((count // SCORE_ROWS,)),
        ],
        compiler_params=pltpu.CompilerParams(vmem_limit_bytes=VMEM_LIMIT),
        name="scores",
    )(*cands, pltpu.with_memory_space_constraint(refs, pltpu.VMEM), *means, *scales)


def per_device(ndb, ncand, coords, species, miller, offsets, form_amps, form_decay, ref_patterns):
    count, nbins = ref_patterns.shape
    held, refs = candidate_patterns(
        coords, species, miller, offsets, form_amps, form_decay, ref_patterns
    )
    members = ndb * ncand
    core = ncand
    masks = [core | ncand << bit for bit in range(1, ndb.bit_length() - 1)]
    masks += [core | 1 << bit for bit in range(ncand.bit_length() - 1)]
    masks.append(core)
    share = -(-count * 5 // 16 // STAT_UNIT) * STAT_UNIT
    cands, means, scales = [held], [], []
    first = 0
    for mask in masks:
        other = lax.ppermute(held, ("db", "cand"), [(i, i ^ mask) for i in range(members)])
        rows = min(share, count - first)
        if rows > 0:
            mean, scale, refs = statistics(refs, first, rows, held)
            means.append(mean)
            scales.append(scale)
            first += rows
            other, mean = lax.optimization_barrier((other, mean))
        cands.append(other)
        held = jnp.concatenate([held, other], axis=0)
    if first < count:
        mean, scale, refs = statistics(refs, first, count - first, held)
        means.append(mean)
        scales.append(scale)
    return score(ncand, tuple(masks), cands, refs, means, scales)


def solution(mesh):
    in_specs = (
        P(None, ("groups", "db", "cand"), None),
        P(("groups", "db", "cand"), None),
        P(),
        P(),
        P(),
        P(),
        P(("db", "cand"), None),
    )
    out_specs = P("groups", ("db", "cand"))
    body = functools.partial(per_device, mesh.shape["db"], mesh.shape["cand"])
    return jax.shard_map(
        body, mesh=mesh, in_specs=in_specs, out_specs=out_specs, check_vma=False
    )
```

```python
import functools

import jax
import jax.numpy as jnp
from jax import lax
from jax.experimental import pallas as pl
from jax.experimental.pallas import tpu as pltpu
from jax.sharding import PartitionSpec as P

EPSILON = 1e-06
Q_SCALE = 0.0025
PEAK_WIDTH = 0.5
LANES = 128
SIDE = 9
POINTS = 96
NORMS = 208
CHUNK = 4096
SCORE_ROWS = 512
STAT_UNIT = 256
STAT_STEP = 256
VMEM_LIMIT = 24 << 20

SIN_COEFS = (3.14159258, -5.1677069, 2.55003164, -0.59804645, 0.07722225)
COS_COEFS = (0.99999995, -4.93479286, 4.05841191, -1.33188016, 0.21969679)


def horner(coefs, x):
    result = coefs[-1] * x + coefs[-2]
    for coef in coefs[-3::-1]:
        result = result * x + coef
    return result


def flat_lanes(rows):
    return jnp.concatenate([rows[c : c + 1] for c in range(rows.shape[0])], axis=1)


def candidate_kernel(
    coords_hbm, species_hbm, miller_hbm, offsets_hbm, amps_hbm, decay_hbm, refs_hbm,
    out_ref, refs_ref,
    coords_ref, species_ref, miller_ref, offsets_ref, amps_ref, decay_ref,
    grid_ref, spread_ref, sems,
):
    sources = (coords_hbm, species_hbm, miller_hbm, offsets_hbm, amps_hbm, decay_hbm, refs_hbm)
    targets = (coords_ref, species_ref, miller_ref, offsets_ref, amps_ref, decay_ref, refs_ref)
    copies = [
        pltpu.make_async_copy(source, target, sems.at[i])
        for i, (source, target) in enumerate(zip(sources, targets))
    ]
    for copy in copies:
        copy.start()
    f32, bf16 = jnp.float32, jnp.bfloat16
    count, atoms = species_ref.shape
    kinds = amps_ref.shape[1]
    reflections = miller_ref.shape[1]
    nbins = out_ref.shape[1]
    nblocks = nbins // LANES
    flat = count * atoms


    axis = lax.broadcasted_iota(jnp.int32, (9, 3 * LANES), 0) // 3
    column = lax.broadcasted_iota(jnp.int32, (9, 3 * LANES), 1)
    tile = column // LANES
    point = column - tile * LANES
    index1 = point // SIDE
    index2 = point - index1 * SIDE
    index2 = jnp.where(tile == 0, index2, -index2)
    yz = jnp.where(axis == 1, index1, jnp.where(axis == 2, index2, 0))
    indices = jnp.where(tile == 2, jnp.where(axis == 0, point, 0), yz)
    indices = indices.astype(f32).astype(bf16)

    point = lax.broadcasted_iota(jnp.int32, (NORMS, LANES), 1)
    index1 = point // SIDE
    index2 = point - index1 * SIDE
    rest = lax.broadcasted_iota(jnp.int32, (NORMS, LANES), 0) - index1 * index1 - index2 * index2
    pick = jnp.concatenate(
        [(rest == h0 * h0).astype(f32).astype(bf16) for h0 in range(SIDE)], axis=1
    )

    centre = lax.broadcasted_iota(jnp.int32, (LANES, 2 * LANES), 0)
    bins = lax.broadcasted_iota(jnp.int32, (LANES, 2 * LANES), 1)
    bins = jnp.where(bins < LANES + LANES // 2, bins, bins - 2 * LANES)
    distance = (bins - centre).astype(f32) * (1.0 / PEAK_WIDTH)
    profile = jnp.exp(-0.5 * distance * distance).astype(bf16)

    for copy in copies[:2] + copies[4:6]:
        copy.wait()
    pieces = []
    for axis in range(3):
        value = flat_lanes(coords_ref[axis])
        for _ in range(3):
            piece = value.astype(bf16)
            value = value - piece.astype(f32)
            pieces.append(piece.astype(f32))
    places = jnp.concatenate(pieces, axis=0).astype(bf16).T

    turns = jnp.dot(places, indices, preferred_element_type=f32)
    u = turns - jnp.round(turns)
    square = u * u
    half_sin = u * horner(SIN_COEFS, square)
    half_cos = horner(COS_COEFS, square)
    cosine = 1.0 - 2.0 * (half_sin * half_sin)
    sine = 2.0 * (half_sin * half_cos)

    norms = lax.broadcasted_iota(jnp.int32, (NORMS, kinds), 0).astype(f32) * Q_SCALE
    table = jnp.zeros((NORMS, kinds), f32)
    for term in range(amps_ref.shape[0]):
        table = table + amps_ref[term : term + 1, :] * jnp.exp(
            -decay_ref[term : term + 1, :] * norms
        )
    onehot = (
        lax.broadcasted_iota(jnp.int32, (kinds, flat), 0) == flat_lanes(species_ref[...])
    ).astype(f32).astype(bf16)
    atom_table = jnp.dot(
        table.astype(bf16), onehot, preferred_element_type=f32
    ).astype(bf16).T
    weight = jnp.dot(atom_table, pick, preferred_element_type=f32)

    points = 2 * SIDE * count
    for c in range(count):
        atom = slice(c * atoms, (c + 1) * atoms)
        for h0 in range(SIDE):
            w = weight[atom, h0 * LANES : (h0 + 1) * LANES]
            w_cos = w * cosine[atom, 2 * LANES + h0 : 2 * LANES + h0 + 1]
            w_sin = w * sine[atom, 2 * LANES + h0 : 2 * LANES + h0 + 1]
            for minus in range(2):
                cos12 = cosine[atom, minus * LANES : (minus + 1) * LANES]
                sin12 = sine[atom, minus * LANES : (minus + 1) * LANES]
                terms = (w_cos * cos12, w_sin * sin12, w_cos * sin12, w_sin * cos12)
                for i, term in enumerate(terms):
                    row = (i * points + (minus * SIDE + h0) * count + c) * 8
                    grid_ref[row : row + 8, :] = jnp.sum(term.reshape(-1, 8, LANES), axis=0)
    cc, ss, cs, sc = (
        sum(grid_ref[pl.ds(i * points * 8 + j, points, stride=8), :] for j in range(8))
        for i in range(4)
    )
    plus = (cc - ss) * (cc - ss) + (cs + sc) * (cs + sc)
    minus = (cc + ss) * (cc + ss) + (cs - sc) * (cs - sc)
    grid = jnp.concatenate([plus, minus], axis=0).astype(bf16)
    group = lax.broadcasted_iota(jnp.int32, (4 * SIDE * count, CHUNK), 0) // count

    for copy in copies[2:4]:
        copy.wait()
    spread_ref[...] = jnp.zeros_like(spread_ref)

    def step(index, carry):
        cols = pl.ds(pl.multiple_of(index * CHUNK, CHUNK), CHUNK)
        miller = miller_ref[:, cols]
        miller = jnp.where(miller[1:2] < 0, -miller, miller)
        size = jnp.abs(miller)
        signs = jnp.where(miller < 0, 1, 0)
        place = size[1:2] * SIDE + size[2:3]
        chosen = (2 * signs[0:1] + signs[2:3]) * SIDE + size[0:1]
        at_place = (
            lax.broadcasted_iota(jnp.int32, (POINTS, CHUNK), 0) == place
        ).astype(f32).astype(bf16)
        values = jnp.dot(grid[:, :POINTS], at_place, preferred_element_type=f32)
        values = jnp.where(group == chosen, values, 0.0)
        intensity = jnp.sum(values.reshape(-1, 8, CHUNK), axis=0)
        shift = count
        while shift < 8:
            intensity = intensity + pltpu.roll(intensity, shift, axis=0)
            shift *= 2

        offset = offsets_ref[:, cols]
        block = offset // LANES
        fold = lax.broadcasted_iota(jnp.int32, (8, CHUNK), 0) // count
        routed = jnp.concatenate(
            [
                jnp.where(block == i + fold, intensity, 0.0)
                for i in range(0, nblocks, 8 // count)
            ],
            axis=0,
        ).astype(bf16)
        local = (
            lax.broadcasted_iota(jnp.int32, (LANES, CHUNK), 0) == offset - block * LANES
        ).astype(f32).astype(bf16)
        spread_ref[...] += lax.dot_general(
            local, routed, (((1,), (1,)), ((), ())), preferred_element_type=f32
        )
        return carry

    lax.fori_loop(0, reflections // CHUNK, step, 0, unroll=True)

    sums = spread_ref[...].T
    pieces = []
    for _ in range(3):
        piece = sums.astype(bf16)
        sums = sums - piece.astype(f32)
        pieces.append(piece.astype(f32))
    peaks = jnp.dot(
        jnp.concatenate(pieces, axis=0).astype(bf16), profile, preferred_element_type=f32
    )
    rows = count * nblocks
    peaks = peaks[:rows] + peaks[rows : 2 * rows] + peaks[2 * rows :]
    lane = lax.broadcasted_iota(jnp.int32, (count, LANES), 1)
    blocks = []
    for i in range(nblocks):
        own = peaks[i * count : (i + 1) * count, :LANES]
        before = after = jnp.zeros_like(own)
        if i > 0:
            before = peaks[(i - 1) * count : i * count, LANES:]
        if i + 1 < nblocks:
            after = peaks[(i + 1) * count : (i + 2) * count, LANES:]
        blocks.append(own + jnp.where(lane < LANES // 2, before, after))
    pattern = jnp.concatenate(blocks, axis=1)
    centered = pattern - jnp.mean(pattern, axis=1, keepdims=True)
    variance = jnp.mean(centered * centered, axis=1, keepdims=True)
    out_ref[...] = (centered / jnp.sqrt(variance + EPSILON)).astype(bf16)
    copies[-1].wait()


def candidate_patterns(coords, species, miller, offsets, form_amps, form_decay, refs):
    count, atoms = species.shape
    nbins = refs.shape[1]
    args = (coords, species, miller, offsets[None, :], form_amps.T, form_decay.T)
    args = [pltpu.with_memory_space_constraint(arg, pltpu.HBM) for arg in args + (refs,)]
    return pl.pallas_call(
        candidate_kernel,
        out_shape=[
            pltpu.VMEM((count, nbins), jnp.bfloat16),
            pltpu.VMEM(refs.shape, refs.dtype),
        ],
        in_specs=[pl.BlockSpec(memory_space=pltpu.HBM)] * len(args),
        scratch_shapes=[pltpu.VMEM(arg.shape, arg.dtype) for arg in args[:-1]]
        + [
            pltpu.VMEM((8 * 8 * SIDE * count, LANES), jnp.float32),
            pltpu.VMEM((LANES, count * (nbins // LANES)), jnp.float32),
            pltpu.SemaphoreType.DMA((len(args),)),
        ],
        compiler_params=pltpu.CompilerParams(vmem_limit_bytes=VMEM_LIMIT),
        name="candidates",
    )(*args)


VMEM_WHOLE = pl.BlockSpec(memory_space=pltpu.VMEM)


def statistics_kernel(first, refs_ref, after_ref, mean_ref, scale_ref, same_ref):
    f32 = jnp.float32
    nbins = refs_ref.shape[1]
    rows = mean_ref.shape[0]
    for at in range(first, first + rows, STAT_STEP):
        tiles = [
            refs_ref[at : at + STAT_STEP, lane : lane + LANES].astype(f32)
            for lane in range(0, nbins, LANES)
        ]
        mean = jnp.sum(sum(tiles[1:], tiles[0]), axis=1, keepdims=True) * (1.0 / nbins)
        total = jnp.zeros((STAT_STEP, LANES), f32)
        for tile in tiles:
            total = total + (tile - mean) * (tile - mean)
        variance = jnp.sum(total, axis=1, keepdims=True) * (1.0 / nbins)
        mean_ref[at - first : at - first + STAT_STEP, :] = mean
        scale_ref[at - first : at - first + STAT_STEP, :] = lax.rsqrt(variance + EPSILON) * (1.0 / nbins**0.5)


def statistics(refs, first, rows, after):
    nbins = refs.shape[1]
    return pl.pallas_call(
        functools.partial(statistics_kernel, first),
        out_shape=[pltpu.VMEM((rows, 1), jnp.float32)] * 2 + [pltpu.VMEM(refs.shape, refs.dtype)],
        in_specs=[VMEM_WHOLE, pl.BlockSpec(memory_space=pl.ANY)],
        out_specs=[VMEM_WHOLE] * 3,
        input_output_aliases={0: 2},
        compiler_params=pltpu.CompilerParams(vmem_limit_bytes=VMEM_LIMIT),
        cost_estimate=pl.CostEstimate(
            flops=2 * rows * nbins * LANES, bytes_accessed=2 * rows * nbins, transcendentals=rows
        ),
        name="statistics",
    )(pltpu.with_memory_space_constraint(refs, pltpu.VMEM), after)


def score_kernel(ncand, masks, npieces, *rest):
    cand_refs, (refs_ref, *rest) = rest[: len(masks) + 1], rest[len(masks) + 1 :]
    mean_refs, scale_refs = rest[:npieces], rest[npieces : 2 * npieces]
    out_ref, cand_t_ref, held_ref, sems = rest[2 * npieces :]
    f32, bf16 = jnp.float32, jnp.bfloat16
    cand = jnp.concatenate([ref[...] for ref in cand_refs], axis=0)
    total, nbins = cand.shape
    block = cand_refs[0].shape[0]
    place = lax.broadcasted_iota(jnp.int32, (total, total), 0)
    group = place // block
    position = lax.axis_index("db") * ncand + lax.axis_index("cand")
    source = jnp.full_like(group, position)
    for bit, mask in enumerate(masks):
        source = source ^ jnp.where((group >> bit) % 2 == 1, mask, 0)
    row = lax.broadcasted_iota(jnp.int32, (total, total), 1)
    order = (row == source * block + place % block).astype(f32).astype(bf16)
    cand_t_ref[...] = lax.dot_general(
        cand, order, (((0,), (0,)), ((), ())), preferred_element_type=f32
    ).astype(bf16)
    sums = jnp.dot(jnp.ones((8, nbins), bf16), cand_t_ref[...], preferred_element_type=f32)[:1]
    means, scales = (
        jnp.concatenate([ref[...] for ref in refs], axis=0) for refs in (mean_refs, scale_refs)
    )
    copies = []
    for i, start in enumerate(range(0, refs_ref.shape[0], SCORE_ROWS)):
        rows = slice(start, start + SCORE_ROWS)
        product = jnp.dot(refs_ref[rows, :], cand_t_ref[...], preferred_element_type=f32)
        product = (product - means[rows] * sums) * scales[rows]
        held_ref[:, rows] = product.T.astype(bf16)
        copy = pltpu.make_async_copy(held_ref.at[:, rows], out_ref.at[:, rows], sems.at[i])
        copy.start()
        copies.append(copy)
    for copy in copies:
        copy.wait()


def score(ncand, masks, cands, refs, means, scales):
    total = sum(cand.shape[0] for cand in cands)
    count, nbins = refs.shape
    return pl.pallas_call(
        functools.partial(score_kernel, ncand, masks, len(means)),
        out_shape=jax.ShapeDtypeStruct((total, count), jnp.bfloat16),
        in_specs=[VMEM_WHOLE] * (len(cands) + 1 + 2 * len(means)),
        out_specs=pl.BlockSpec(memory_space=pltpu.HBM),
        scratch_shapes=[
            pltpu.VMEM((nbins, total), jnp.bfloat16),
            pltpu.VMEM((total, count), jnp.bfloat16),
            pltpu.SemaphoreType.DMA((count // SCORE_ROWS,)),
        ],
        compiler_params=pltpu.CompilerParams(vmem_limit_bytes=VMEM_LIMIT),
        name="scores",
    )(*cands, pltpu.with_memory_space_constraint(refs, pltpu.VMEM), *means, *scales)


def per_device(ndb, ncand, coords, species, miller, offsets, form_amps, form_decay, ref_patterns):
    count, nbins = ref_patterns.shape
    held, refs = candidate_patterns(
        coords, species, miller, offsets, form_amps, form_decay, ref_patterns
    )
    members = ndb * ncand
    core = ncand
    masks = [core | 1 << bit for bit in reversed(range(ncand.bit_length() - 1))]
    masks += [core | ncand << bit for bit in range(1, ndb.bit_length() - 1)]
    masks.append(core)
    share = -(-count * 5 // 16 // STAT_UNIT) * STAT_UNIT
    cands, means, scales = [held], [], []
    first = 0
    for mask in masks:
        other = lax.ppermute(held, ("db", "cand"), [(i, i ^ mask) for i in range(members)])
        rows = min(share, count - first)
        if rows > 0:
            mean, scale, refs = statistics(refs, first, rows, held)
            means.append(mean)
            scales.append(scale)
            first += rows
            other, mean = lax.optimization_barrier((other, mean))
        cands.append(other)
        held = jnp.concatenate([held, other], axis=0)
    if first < count:
        mean, scale, refs = statistics(refs, first, count - first, held)
        means.append(mean)
        scales.append(scale)
    return score(ncand, tuple(masks), cands, refs, means, scales)


def solution(mesh):
    in_specs = (
        P(None, ("groups", "db", "cand"), None),
        P(("groups", "db", "cand"), None),
        P(),
        P(),
        P(),
        P(),
        P(("db", "cand"), None),
    )
    out_specs = P("groups", ("db", "cand"))
    body = functools.partial(per_device, mesh.shape["db"], mesh.shape["cand"])
    return jax.shard_map(
        body, mesh=mesh, in_specs=in_specs, out_specs=out_specs, check_vma=False
    )
```

```python
import functools

import jax
import jax.numpy as jnp
from jax import lax
from jax.experimental import pallas as pl
from jax.experimental.pallas import tpu as pltpu
from jax.sharding import PartitionSpec as P

EPSILON = 1e-06
Q_SCALE = 0.0025
PEAK_WIDTH = 0.5
LANES = 128
SIDE = 9
POINTS = 96
NORMS = 208
CHUNK = 4096
SCORE_ROWS = 512
STAT_UNIT = 256
STAT_STEP = 256
VMEM_LIMIT = 24 << 20

SIN_COEFS = (3.14159258, -5.1677069, 2.55003164, -0.59804645, 0.07722225)
COS_COEFS = (0.99999995, -4.93479286, 4.05841191, -1.33188016, 0.21969679)


def horner(coefs, x):
    result = coefs[-1] * x + coefs[-2]
    for coef in coefs[-3::-1]:
        result = result * x + coef
    return result


def flat_lanes(rows):
    return jnp.concatenate([rows[c : c + 1] for c in range(rows.shape[0])], axis=1)


def candidate_kernel(
    coords_hbm, species_hbm, miller_hbm, offsets_hbm, amps_hbm, decay_hbm, refs_hbm,
    out_ref, refs_ref,
    coords_ref, species_ref, miller_ref, offsets_ref, amps_ref, decay_ref,
    grid_ref, spread_ref, sems,
):
    sources = (coords_hbm, species_hbm, miller_hbm, offsets_hbm, amps_hbm, decay_hbm, refs_hbm)
    targets = (coords_ref, species_ref, miller_ref, offsets_ref, amps_ref, decay_ref, refs_ref)
    copies = [
        pltpu.make_async_copy(source, target, sems.at[i])
        for i, (source, target) in enumerate(zip(sources, targets))
    ]
    for copy in copies:
        copy.start()
    f32, bf16 = jnp.float32, jnp.bfloat16
    count, atoms = species_ref.shape
    kinds = amps_ref.shape[1]
    reflections = miller_ref.shape[1]
    nbins = out_ref.shape[1]
    nblocks = nbins // LANES
    flat = count * atoms


    axis = lax.broadcasted_iota(jnp.int32, (9, 3 * LANES), 0) // 3
    column = lax.broadcasted_iota(jnp.int32, (9, 3 * LANES), 1)
    tile = column // LANES
    point = column - tile * LANES
    index1 = point // SIDE
    index2 = point - index1 * SIDE
    index2 = jnp.where(tile == 0, index2, -index2)
    yz = jnp.where(axis == 1, index1, jnp.where(axis == 2, index2, 0))
    indices = jnp.where(tile == 2, jnp.where(axis == 0, point, 0), yz)
    indices = indices.astype(f32).astype(bf16)

    point = lax.broadcasted_iota(jnp.int32, (NORMS, LANES), 1)
    index1 = point // SIDE
    index2 = point - index1 * SIDE
    rest = lax.broadcasted_iota(jnp.int32, (NORMS, LANES), 0) - index1 * index1 - index2 * index2
    pick = jnp.concatenate(
        [(rest == h0 * h0).astype(f32).astype(bf16) for h0 in range(SIDE)], axis=1
    )

    centre = lax.broadcasted_iota(jnp.int32, (LANES, 2 * LANES), 0)
    bins = lax.broadcasted_iota(jnp.int32, (LANES, 2 * LANES), 1)
    bins = jnp.where(bins < LANES + LANES // 2, bins, bins - 2 * LANES)
    distance = (bins - centre).astype(f32) * (1.0 / PEAK_WIDTH)
    profile = jnp.exp(-0.5 * distance * distance).astype(bf16)

    for copy in copies[:2] + copies[4:6]:
        copy.wait()
    pieces = []
    for axis in range(3):
        value = flat_lanes(coords_ref[axis])
        for _ in range(3):
            piece = value.astype(bf16)
            value = value - piece.astype(f32)
            pieces.append(piece.astype(f32))
    places = jnp.concatenate(pieces, axis=0).astype(bf16).T

    turns = jnp.dot(places, indices, preferred_element_type=f32)
    u = turns - jnp.round(turns)
    square = u * u
    half_sin = u * horner(SIN_COEFS, square)
    half_cos = horner(COS_COEFS, square)
    cosine = 1.0 - 2.0 * (half_sin * half_sin)
    sine = 2.0 * (half_sin * half_cos)

    norms = lax.broadcasted_iota(jnp.int32, (NORMS, kinds), 0).astype(f32) * Q_SCALE
    table = jnp.zeros((NORMS, kinds), f32)
    for term in range(amps_ref.shape[0]):
        table = table + amps_ref[term : term + 1, :] * jnp.exp(
            -decay_ref[term : term + 1, :] * norms
        )
    onehot = (
        lax.broadcasted_iota(jnp.int32, (kinds, flat), 0) == flat_lanes(species_ref[...])
    ).astype(f32).astype(bf16)
    atom_table = jnp.dot(
        table.astype(bf16), onehot, preferred_element_type=f32
    ).astype(bf16).T
    weight = jnp.dot(atom_table, pick, preferred_element_type=f32)

    points = 2 * SIDE * count
    for c in range(count):
        atom = slice(c * atoms, (c + 1) * atoms)
        for h0 in range(SIDE):
            w = weight[atom, h0 * LANES : (h0 + 1) * LANES]
            w_cos = w * cosine[atom, 2 * LANES + h0 : 2 * LANES + h0 + 1]
            w_sin = w * sine[atom, 2 * LANES + h0 : 2 * LANES + h0 + 1]
            for minus in range(2):
                cos12 = cosine[atom, minus * LANES : (minus + 1) * LANES]
                sin12 = sine[atom, minus * LANES : (minus + 1) * LANES]
                terms = (w_cos * cos12, w_sin * sin12, w_cos * sin12, w_sin * cos12)
                for i, term in enumerate(terms):
                    row = (i * points + (minus * SIDE + h0) * count + c) * 8
                    grid_ref[row : row + 8, :] = jnp.sum(term.reshape(-1, 8, LANES), axis=0)
    cc, ss, cs, sc = (
        sum(grid_ref[pl.ds(i * points * 8 + j, points, stride=8), :] for j in range(8))
        for i in range(4)
    )
    plus = (cc - ss) * (cc - ss) + (cs + sc) * (cs + sc)
    minus = (cc + ss) * (cc + ss) + (cs - sc) * (cs - sc)
    grid = jnp.concatenate([plus, minus], axis=0).astype(bf16)
    group = lax.broadcasted_iota(jnp.int32, (4 * SIDE * count, CHUNK), 0) // count

    for copy in copies[2:4]:
        copy.wait()
    spread_ref[...] = jnp.zeros_like(spread_ref)

    def step(index, carry):
        cols = pl.ds(pl.multiple_of(index * CHUNK, CHUNK), CHUNK)
        miller = miller_ref[:, cols]
        miller = jnp.where(miller[1:2] < 0, -miller, miller)
        size = jnp.abs(miller)
        signs = jnp.where(miller < 0, 1, 0)
        place = size[1:2] * SIDE + size[2:3]
        chosen = (2 * signs[0:1] + signs[2:3]) * SIDE + size[0:1]
        at_place = (
            lax.broadcasted_iota(jnp.int32, (POINTS, CHUNK), 0) == place
        ).astype(f32).astype(bf16)
        values = jnp.dot(grid[:, :POINTS], at_place, preferred_element_type=f32)
        values = jnp.where(group == chosen, values, 0.0)
        intensity = jnp.sum(values.reshape(-1, 8, CHUNK), axis=0)
        shift = count
        while shift < 8:
            intensity = intensity + pltpu.roll(intensity, shift, axis=0)
            shift *= 2

        offset = offsets_ref[:, cols]
        block = offset // LANES
        fold = lax.broadcasted_iota(jnp.int32, (8, CHUNK), 0) // count
        routed = jnp.concatenate(
            [
                jnp.where(block == i + fold, intensity, 0.0)
                for i in range(0, nblocks, 8 // count)
            ],
            axis=0,
        ).astype(bf16)
        local = (
            lax.broadcasted_iota(jnp.int32, (LANES, CHUNK), 0) == offset - block * LANES
        ).astype(f32).astype(bf16)
        spread_ref[...] += lax.dot_general(
            local, routed, (((1,), (1,)), ((), ())), preferred_element_type=f32
        )
        return carry

    lax.fori_loop(0, reflections // CHUNK, step, 0, unroll=True)

    sums = spread_ref[...].T
    pieces = []
    for _ in range(3):
        piece = sums.astype(bf16)
        sums = sums - piece.astype(f32)
        pieces.append(piece.astype(f32))
    peaks = jnp.dot(
        jnp.concatenate(pieces, axis=0).astype(bf16), profile, preferred_element_type=f32
    )
    rows = count * nblocks
    peaks = peaks[:rows] + peaks[rows : 2 * rows] + peaks[2 * rows :]
    lane = lax.broadcasted_iota(jnp.int32, (count, LANES), 1)
    blocks = []
    for i in range(nblocks):
        own = peaks[i * count : (i + 1) * count, :LANES]
        before = after = jnp.zeros_like(own)
        if i > 0:
            before = peaks[(i - 1) * count : i * count, LANES:]
        if i + 1 < nblocks:
            after = peaks[(i + 1) * count : (i + 2) * count, LANES:]
        blocks.append(own + jnp.where(lane < LANES // 2, before, after))
    pattern = jnp.concatenate(blocks, axis=1)
    centered = pattern - jnp.mean(pattern, axis=1, keepdims=True)
    variance = jnp.mean(centered * centered, axis=1, keepdims=True)
    out_ref[...] = (centered / jnp.sqrt(variance + EPSILON)).astype(bf16)
    copies[-1].wait()


def candidate_patterns(coords, species, miller, offsets, form_amps, form_decay, refs):
    count, atoms = species.shape
    nbins = refs.shape[1]
    args = (coords, species, miller, offsets[None, :], form_amps.T, form_decay.T)
    args = [pltpu.with_memory_space_constraint(arg, pltpu.HBM) for arg in args + (refs,)]
    return pl.pallas_call(
        candidate_kernel,
        out_shape=[
            pltpu.VMEM((count, nbins), jnp.bfloat16),
            pltpu.VMEM(refs.shape, refs.dtype),
        ],
        in_specs=[pl.BlockSpec(memory_space=pltpu.HBM)] * len(args),
        scratch_shapes=[pltpu.VMEM(arg.shape, arg.dtype) for arg in args[:-1]]
        + [
            pltpu.VMEM((8 * 8 * SIDE * count, LANES), jnp.float32),
            pltpu.VMEM((LANES, count * (nbins // LANES)), jnp.float32),
            pltpu.SemaphoreType.DMA((len(args),)),
        ],
        compiler_params=pltpu.CompilerParams(vmem_limit_bytes=VMEM_LIMIT),
        name="candidates",
    )(*args)


VMEM_WHOLE = pl.BlockSpec(memory_space=pltpu.VMEM)


def statistics_kernel(first, refs_ref, after_ref, mean_ref, scale_ref, same_ref):
    f32 = jnp.float32
    nbins = refs_ref.shape[1]
    rows = mean_ref.shape[0]
    for at in range(first, first + rows, STAT_STEP):
        tiles = [
            refs_ref[at : at + STAT_STEP, lane : lane + LANES].astype(f32)
            for lane in range(0, nbins, LANES)
        ]
        mean = jnp.sum(sum(tiles[1:], tiles[0]), axis=1, keepdims=True) * (1.0 / nbins)
        total = jnp.zeros((STAT_STEP, LANES), f32)
        for tile in tiles:
            total = total + (tile - mean) * (tile - mean)
        variance = jnp.sum(total, axis=1, keepdims=True) * (1.0 / nbins)
        mean_ref[at - first : at - first + STAT_STEP, :] = mean
        scale_ref[at - first : at - first + STAT_STEP, :] = lax.rsqrt(variance + EPSILON) * (1.0 / nbins**0.5)


def statistics(refs, first, rows, after):
    nbins = refs.shape[1]
    return pl.pallas_call(
        functools.partial(statistics_kernel, first),
        out_shape=[pltpu.VMEM((rows, 1), jnp.float32)] * 2 + [pltpu.VMEM(refs.shape, refs.dtype)],
        in_specs=[VMEM_WHOLE, pl.BlockSpec(memory_space=pl.ANY)],
        out_specs=[VMEM_WHOLE] * 3,
        input_output_aliases={0: 2},
        compiler_params=pltpu.CompilerParams(vmem_limit_bytes=VMEM_LIMIT),
        cost_estimate=pl.CostEstimate(
            flops=2 * rows * nbins * LANES, bytes_accessed=2 * rows * nbins, transcendentals=rows
        ),
        name="statistics",
    )(pltpu.with_memory_space_constraint(refs, pltpu.VMEM), after)


def score_kernel(ncand, masks, npieces, held_ref, other_ref, refs_ref, *rest):
    mean_refs, scale_refs = rest[:npieces], rest[npieces : 2 * npieces]
    out_ref, scores_ref, sems = rest[2 * npieces :]
    f32, bf16 = jnp.float32, jnp.bfloat16
    cand = jnp.concatenate([held_ref[...], other_ref[...]], axis=0)
    total, nbins = cand.shape
    block = total >> len(masks)
    last = (((1,), (1,)), ((), ()))
    place = lax.broadcasted_iota(jnp.int32, (total, total), 1)
    group = place // block
    position = lax.axis_index("db") * ncand + lax.axis_index("cand")
    source = jnp.full_like(group, position)
    for bit, mask in enumerate(masks):
        source = source ^ jnp.where((group >> bit) % 2 == 1, mask, 0)
    row = lax.broadcasted_iota(jnp.int32, (total, total), 0)
    order = (row == source * block + place % block).astype(f32).astype(bf16)
    cand = jnp.dot(order, cand, preferred_element_type=f32).astype(bf16)
    sums = lax.dot_general(jnp.ones((8, nbins), bf16), cand, last, preferred_element_type=f32)[:1]
    means, scales = (
        jnp.concatenate([ref[...] for ref in refs], axis=0) for refs in (mean_refs, scale_refs)
    )
    copies = []
    for i, start in enumerate(range(0, refs_ref.shape[0], SCORE_ROWS)):
        rows = slice(start, start + SCORE_ROWS)
        product = lax.dot_general(refs_ref[rows, :], cand, last, preferred_element_type=f32)
        product = (product - means[rows] * sums) * scales[rows]
        scores_ref[:, rows] = product.T.astype(bf16)
        copy = pltpu.make_async_copy(scores_ref.at[:, rows], out_ref.at[:, rows], sems.at[i])
        copy.start()
        copies.append(copy)
    for copy in copies:
        copy.wait()


def score(ncand, masks, held, other, refs, means, scales):
    total = held.shape[0] + other.shape[0]
    count = refs.shape[0]
    return pl.pallas_call(
        functools.partial(score_kernel, ncand, masks, len(means)),
        out_shape=jax.ShapeDtypeStruct((total, count), jnp.bfloat16),
        in_specs=[VMEM_WHOLE] * (3 + 2 * len(means)),
        out_specs=pl.BlockSpec(memory_space=pltpu.HBM),
        scratch_shapes=[
            pltpu.VMEM((total, count), jnp.bfloat16),
            pltpu.SemaphoreType.DMA((count // SCORE_ROWS,)),
        ],
        compiler_params=pltpu.CompilerParams(vmem_limit_bytes=VMEM_LIMIT),
        name="scores",
    )(held, other, pltpu.with_memory_space_constraint(refs, pltpu.VMEM), *means, *scales)


def per_device(ndb, ncand, coords, species, miller, offsets, form_amps, form_decay, ref_patterns):
    count, nbins = ref_patterns.shape
    held, refs = candidate_patterns(
        coords, species, miller, offsets, form_amps, form_decay, ref_patterns
    )
    members = ndb * ncand
    core = ncand
    masks = [core | 1 << bit for bit in reversed(range(ncand.bit_length() - 1))]
    masks += [core | ncand << bit for bit in range(1, ndb.bit_length() - 1)]
    masks.append(core)
    share = -(-count * 5 // 16 // STAT_UNIT) * STAT_UNIT
    means, scales = [], []
    first = 0
    for mask in masks:
        other = lax.ppermute(held, ("db", "cand"), [(i, i ^ mask) for i in range(members)])
        rows = min(share, count - first)
        if rows > 0:
            mean, scale, refs = statistics(refs, first, rows, held)
            means.append(mean)
            scales.append(scale)
            first += rows
            other, mean = lax.optimization_barrier((other, mean))
        if mask != core:
            held = jnp.concatenate([held, other], axis=0)
    if first < count:
        mean, scale, refs = statistics(refs, first, count - first, held)
        means.append(mean)
        scales.append(scale)
    return score(ncand, tuple(masks), held, other, refs, means, scales)


def solution(mesh):
    in_specs = (
        P(None, ("groups", "db", "cand"), None),
        P(("groups", "db", "cand"), None),
        P(),
        P(),
        P(),
        P(),
        P(("db", "cand"), None),
    )
    out_specs = P("groups", ("db", "cand"))
    body = functools.partial(per_device, mesh.shape["db"], mesh.shape["cand"])
    return jax.shard_map(
        body, mesh=mesh, in_specs=in_specs, out_specs=out_specs, check_vma=False
    )
```

```python
import functools

import jax
import jax.numpy as jnp
from jax import lax
from jax.experimental import pallas as pl
from jax.experimental.pallas import tpu as pltpu
from jax.sharding import PartitionSpec as P

EPSILON = 1e-06
Q_SCALE = 0.0025
PEAK_WIDTH = 0.5
LANES = 128
SIDE = 9
POINTS = 96
NORMS = 208
CHUNK = 4096
SCORE_ROWS = 512
STAT_UNIT = 256
STAT_STEP = 256
VMEM_LIMIT = 24 << 20

SIN_COEFS = (3.14159258, -5.1677069, 2.55003164, -0.59804645, 0.07722225)
COS_COEFS = (0.99999995, -4.93479286, 4.05841191, -1.33188016, 0.21969679)


def horner(coefs, x):
    result = coefs[-1] * x + coefs[-2]
    for coef in coefs[-3::-1]:
        result = result * x + coef
    return result


def flat_lanes(rows):
    return jnp.concatenate([rows[c : c + 1] for c in range(rows.shape[0])], axis=1)


def candidate_kernel(
    coords_hbm, species_hbm, miller_hbm, offsets_hbm, amps_hbm, decay_hbm, refs_hbm,
    out_ref, refs_ref,
    coords_ref, species_ref, miller_ref, offsets_ref, amps_ref, decay_ref,
    grid_ref, spread_ref, sems,
):
    sources = (coords_hbm, species_hbm, amps_hbm, decay_hbm, miller_hbm, offsets_hbm, refs_hbm)
    targets = (coords_ref, species_ref, amps_ref, decay_ref, miller_ref, offsets_ref, refs_ref)
    copies = [
        pltpu.make_async_copy(source, target, sems.at[i])
        for i, (source, target) in enumerate(zip(sources, targets))
    ]
    for copy in copies:
        copy.start()
    f32, bf16 = jnp.float32, jnp.bfloat16
    count, atoms = species_ref.shape
    kinds = amps_ref.shape[1]
    reflections = miller_ref.shape[1]
    nbins = out_ref.shape[1]
    nblocks = nbins // LANES
    flat = count * atoms

    axis = lax.broadcasted_iota(jnp.int32, (9, 3 * LANES), 0) // 3
    column = lax.broadcasted_iota(jnp.int32, (9, 3 * LANES), 1)
    tile = column // LANES
    point = column - tile * LANES
    index1 = point // SIDE
    index2 = point - index1 * SIDE
    index2 = jnp.where(tile == 0, index2, -index2)
    yz = jnp.where(axis == 1, index1, jnp.where(axis == 2, index2, 0))
    indices = jnp.where(tile == 2, jnp.where(axis == 0, point, 0), yz)
    indices = indices.astype(f32).astype(bf16)

    point = lax.broadcasted_iota(jnp.int32, (NORMS, LANES), 1)
    index1 = point // SIDE
    index2 = point - index1 * SIDE
    rest = lax.broadcasted_iota(jnp.int32, (NORMS, LANES), 0) - index1 * index1 - index2 * index2
    pick = jnp.concatenate(
        [(rest == h0 * h0).astype(f32).astype(bf16) for h0 in range(SIDE)], axis=1
    )

    centre = lax.broadcasted_iota(jnp.int32, (LANES, 2 * LANES), 0)
    bins = lax.broadcasted_iota(jnp.int32, (LANES, 2 * LANES), 1)
    bins = jnp.where(bins < LANES + LANES // 2, bins, bins - 2 * LANES)
    distance = (bins - centre).astype(f32) * (1.0 / PEAK_WIDTH)
    profile = jnp.exp(-0.5 * distance * distance).astype(bf16)
    for copy in copies[:4]:
        copy.wait()
    pieces = []
    for axis in range(3):
        value = flat_lanes(coords_ref[axis])
        for _ in range(3):
            piece = value.astype(bf16)
            value = value - piece.astype(f32)
            pieces.append(piece.astype(f32))
    places = jnp.concatenate(pieces, axis=0).astype(bf16).T

    turns = jnp.dot(places, indices, preferred_element_type=f32)
    u = turns - jnp.round(turns)
    square = u * u
    half_sin = u * horner(SIN_COEFS, square)
    half_cos = horner(COS_COEFS, square)
    cosine = 1.0 - 2.0 * (half_sin * half_sin)
    sine = 2.0 * (half_sin * half_cos)

    norms = lax.broadcasted_iota(jnp.int32, (NORMS, kinds), 0).astype(f32) * Q_SCALE
    table = jnp.zeros((NORMS, kinds), f32)
    for term in range(amps_ref.shape[0]):
        table = table + amps_ref[term : term + 1, :] * jnp.exp(
            -decay_ref[term : term + 1, :] * norms
        )
    onehot = (
        lax.broadcasted_iota(jnp.int32, (kinds, flat), 0) == flat_lanes(species_ref[...])
    ).astype(f32).astype(bf16)
    atom_table = jnp.dot(
        table.astype(bf16), onehot, preferred_element_type=f32
    ).astype(bf16).T
    weight = jnp.dot(atom_table, pick, preferred_element_type=f32)

    points = 2 * SIDE * count
    for c in range(count):
        atom = slice(c * atoms, (c + 1) * atoms)
        for h0 in range(SIDE):
            w = weight[atom, h0 * LANES : (h0 + 1) * LANES]
            w_cos = w * cosine[atom, 2 * LANES + h0 : 2 * LANES + h0 + 1]
            w_sin = w * sine[atom, 2 * LANES + h0 : 2 * LANES + h0 + 1]
            for minus in range(2):
                cos12 = cosine[atom, minus * LANES : (minus + 1) * LANES]
                sin12 = sine[atom, minus * LANES : (minus + 1) * LANES]
                terms = (w_cos * cos12, w_sin * sin12, w_cos * sin12, w_sin * cos12)
                for i, term in enumerate(terms):
                    row = (i * points + (minus * SIDE + h0) * count + c) * 8
                    grid_ref[row : row + 8, :] = jnp.sum(term.reshape(-1, 8, LANES), axis=0)
    cc, ss, cs, sc = (
        sum(grid_ref[pl.ds(i * points * 8 + j, points, stride=8), :] for j in range(8))
        for i in range(4)
    )
    plus = (cc - ss) * (cc - ss) + (cs + sc) * (cs + sc)
    minus = (cc + ss) * (cc + ss) + (cs - sc) * (cs - sc)
    grid = jnp.concatenate([plus, minus], axis=0).astype(bf16)
    group = lax.broadcasted_iota(jnp.int32, (4 * SIDE * count, CHUNK), 0) // count

    for copy in copies[4:6]:
        copy.wait()
    spread_ref[...] = jnp.zeros_like(spread_ref)

    def step(index, carry):
        cols = pl.ds(pl.multiple_of(index * CHUNK, CHUNK), CHUNK)
        miller = miller_ref[:, cols]
        miller = jnp.where(miller[1:2] < 0, -miller, miller)
        size = jnp.abs(miller)
        signs = jnp.where(miller < 0, 1, 0)
        place = size[1:2] * SIDE + size[2:3]
        chosen = (2 * signs[0:1] + signs[2:3]) * SIDE + size[0:1]
        at_place = (
            lax.broadcasted_iota(jnp.int32, (POINTS, CHUNK), 0) == place
        ).astype(f32).astype(bf16)
        values = jnp.dot(grid[:, :POINTS], at_place, preferred_element_type=f32)
        values = jnp.where(group == chosen, values, 0.0)
        intensity = jnp.sum(values.reshape(-1, 8, CHUNK), axis=0)
        shift = count
        while shift < 8:
            intensity = intensity + pltpu.roll(intensity, shift, axis=0)
            shift *= 2

        offset = offsets_ref[:, cols]
        block = offset // LANES
        fold = lax.broadcasted_iota(jnp.int32, (8, CHUNK), 0) // count
        routed = jnp.concatenate(
            [
                jnp.where(block == i + fold, intensity, 0.0)
                for i in range(0, nblocks, 8 // count)
            ],
            axis=0,
        ).astype(bf16)
        local = (
            lax.broadcasted_iota(jnp.int32, (LANES, CHUNK), 0) == offset - block * LANES
        ).astype(f32).astype(bf16)
        spread_ref[...] += lax.dot_general(
            local, routed, (((1,), (1,)), ((), ())), preferred_element_type=f32
        )
        return carry

    lax.fori_loop(0, reflections // CHUNK, step, 0, unroll=True)

    sums = spread_ref[...].T
    pieces = []
    for _ in range(3):
        pieces.append(sums.astype(bf16))
        sums = sums - pieces[-1].astype(f32)
    peaks = jnp.dot(
        jnp.concatenate(pieces, axis=1),
        jnp.concatenate([profile] * 3, axis=0),
        preferred_element_type=f32,
    )
    lane = lax.broadcasted_iota(jnp.int32, (count, LANES), 1)
    blocks = []
    for i in range(nblocks):
        own = peaks[i * count : (i + 1) * count, :LANES]
        before = after = jnp.zeros_like(own)
        if i > 0:
            before = peaks[(i - 1) * count : i * count, LANES:]
        if i + 1 < nblocks:
            after = peaks[(i + 1) * count : (i + 2) * count, LANES:]
        blocks.append(own + jnp.where(lane < LANES // 2, before, after))
    pattern = jnp.concatenate(blocks, axis=1)
    centered = pattern - jnp.mean(pattern, axis=1, keepdims=True)
    variance = jnp.mean(centered * centered, axis=1, keepdims=True)
    out_ref[...] = (centered / jnp.sqrt(variance + EPSILON)).astype(bf16)
    copies[-1].wait()


def candidate_patterns(coords, species, miller, offsets, form_amps, form_decay, refs):
    count, atoms = species.shape
    nbins = refs.shape[1]
    args = (coords, species, miller, offsets[None, :], form_amps.T, form_decay.T)
    args = [pltpu.with_memory_space_constraint(arg, pltpu.HBM) for arg in args + (refs,)]
    return pl.pallas_call(
        candidate_kernel,
        out_shape=[
            pltpu.VMEM((count, nbins), jnp.bfloat16),
            pltpu.VMEM(refs.shape, refs.dtype),
        ],
        in_specs=[pl.BlockSpec(memory_space=pltpu.HBM)] * len(args),
        scratch_shapes=[pltpu.VMEM(arg.shape, arg.dtype) for arg in args[:-1]]
        + [
            pltpu.VMEM((8 * 8 * SIDE * count + 8, LANES), jnp.float32),
            pltpu.VMEM((LANES, count * (nbins // LANES)), jnp.float32),
            pltpu.SemaphoreType.DMA((len(args),)),
        ],
        compiler_params=pltpu.CompilerParams(vmem_limit_bytes=VMEM_LIMIT),
        name="candidates",
    )(*args)


VMEM_WHOLE = pl.BlockSpec(memory_space=pltpu.VMEM)


def statistics_kernel(first, refs_ref, after_ref, mean_ref, scale_ref, same_ref):
    f32 = jnp.float32
    nbins = refs_ref.shape[1]
    rows = mean_ref.shape[0]
    for at in range(first, first + rows, STAT_STEP):
        tiles = [
            refs_ref[at : at + STAT_STEP, lane : lane + LANES].astype(f32)
            for lane in range(0, nbins, LANES)
        ]
        mean = jnp.sum(sum(tiles[1:], tiles[0]), axis=1, keepdims=True) * (1.0 / nbins)
        total = jnp.zeros((STAT_STEP, LANES), f32)
        for tile in tiles:
            total = total + (tile - mean) * (tile - mean)
        variance = jnp.sum(total, axis=1, keepdims=True) * (1.0 / nbins)
        mean_ref[at - first : at - first + STAT_STEP, :] = mean
        scale_ref[at - first : at - first + STAT_STEP, :] = lax.rsqrt(variance + EPSILON) * (1.0 / nbins**0.5)


def statistics(refs, first, rows, after):
    nbins = refs.shape[1]
    return pl.pallas_call(
        functools.partial(statistics_kernel, first),
        out_shape=[pltpu.VMEM((rows, 1), jnp.float32)] * 2 + [pltpu.VMEM(refs.shape, refs.dtype)],
        in_specs=[VMEM_WHOLE, pl.BlockSpec(memory_space=pl.ANY)],
        out_specs=[VMEM_WHOLE] * 3,
        input_output_aliases={0: 2},
        compiler_params=pltpu.CompilerParams(vmem_limit_bytes=VMEM_LIMIT),
        cost_estimate=pl.CostEstimate(
            flops=2 * rows * nbins * LANES, bytes_accessed=2 * rows * nbins, transcendentals=rows
        ),
        name="statistics",
    )(pltpu.with_memory_space_constraint(refs, pltpu.VMEM), after)


def score_kernel(ncand, masks, npieces, held_ref, other_ref, refs_ref, *rest):
    mean_refs, scale_refs = rest[:npieces], rest[npieces : 2 * npieces]
    out_ref, scores_ref, sems = rest[2 * npieces :]
    f32, bf16 = jnp.float32, jnp.bfloat16
    cand = jnp.concatenate([held_ref[...], other_ref[...]], axis=0)
    total, nbins = cand.shape
    block = total >> len(masks)
    last = (((1,), (1,)), ((), ()))
    place = lax.broadcasted_iota(jnp.int32, (total, total), 1)
    group = place // block
    position = lax.axis_index("db") * ncand + lax.axis_index("cand")
    source = jnp.full_like(group, position)
    for bit, mask in enumerate(masks):
        source = source ^ jnp.where((group >> bit) % 2 == 1, mask, 0)
    row = lax.broadcasted_iota(jnp.int32, (total, total), 0)
    order = (row == source * block + place % block).astype(f32).astype(bf16)
    cand = jnp.dot(order, cand, preferred_element_type=f32).astype(bf16)
    sums = lax.dot_general(jnp.ones((8, nbins), bf16), cand, last, preferred_element_type=f32)[:1]
    means, scales = (
        jnp.concatenate([ref[...] for ref in refs], axis=0) for refs in (mean_refs, scale_refs)
    )
    copies = []
    for i, start in enumerate(range(0, refs_ref.shape[0], SCORE_ROWS)):
        rows = slice(start, start + SCORE_ROWS)
        product = lax.dot_general(refs_ref[rows, :], cand, last, preferred_element_type=f32)
        product = (product - means[rows] * sums) * scales[rows]
        scores_ref[:, rows] = product.T.astype(bf16)
        copy = pltpu.make_async_copy(scores_ref.at[:, rows], out_ref.at[:, rows], sems.at[i])
        copy.start()
        copies.append(copy)
    for copy in copies:
        copy.wait()


def score(ncand, masks, held, other, refs, means, scales):
    total = held.shape[0] + other.shape[0]
    count = refs.shape[0]
    return pl.pallas_call(
        functools.partial(score_kernel, ncand, masks, len(means)),
        out_shape=jax.ShapeDtypeStruct((total, count), jnp.bfloat16),
        in_specs=[VMEM_WHOLE] * (3 + 2 * len(means)),
        out_specs=pl.BlockSpec(memory_space=pltpu.HBM),
        scratch_shapes=[
            pltpu.VMEM((total, count), jnp.bfloat16),
            pltpu.SemaphoreType.DMA((count // SCORE_ROWS,)),
        ],
        compiler_params=pltpu.CompilerParams(vmem_limit_bytes=VMEM_LIMIT),
        name="scores",
    )(held, other, pltpu.with_memory_space_constraint(refs, pltpu.VMEM), *means, *scales)


def per_device(ndb, ncand, coords, species, miller, offsets, form_amps, form_decay, ref_patterns):
    count, nbins = ref_patterns.shape
    held, refs = candidate_patterns(
        coords, species, miller, offsets, form_amps, form_decay, ref_patterns
    )
    members = ndb * ncand
    core = ncand
    masks = [core | 1 << bit for bit in reversed(range(ncand.bit_length() - 1))]
    masks += [core | ncand << bit for bit in range(1, ndb.bit_length() - 1)]
    masks.append(core)
    share = -(-count * 5 // 16 // STAT_UNIT) * STAT_UNIT
    means, scales = [], []
    first = 0
    for mask in masks:
        other = lax.ppermute(held, ("db", "cand"), [(i, i ^ mask) for i in range(members)])
        rows = min(share, count - first)
        if rows > 0:
            mean, scale, refs = statistics(refs, first, rows, held)
            means.append(mean)
            scales.append(scale)
            first += rows
            other, mean = lax.optimization_barrier((other, mean))
        if mask != core:
            held = jnp.concatenate([held, other], axis=0)
    if first < count:
        mean, scale, refs = statistics(refs, first, count - first, held)
        means.append(mean)
        scales.append(scale)
    return score(ncand, tuple(masks), held, other, refs, means, scales)


def solution(mesh):
    in_specs = (
        P(None, ("groups", "db", "cand"), None),
        P(("groups", "db", "cand"), None),
        P(),
        P(),
        P(),
        P(),
        P(("db", "cand"), None),
    )
    out_specs = P("groups", ("db", "cand"))
    body = functools.partial(per_device, mesh.shape["db"], mesh.shape["cand"])
    return jax.shard_map(
        body, mesh=mesh, in_specs=in_specs, out_specs=out_specs, check_vma=False
    )
```

```python
import functools

import jax
import jax.numpy as jnp
from jax import lax
from jax.experimental import pallas as pl
from jax.experimental.pallas import tpu as pltpu
from jax.sharding import PartitionSpec as P

EPSILON = 1e-06
Q_SCALE = 0.0025
PEAK_WIDTH = 0.5
LANES = 128
SIDE = 9
POINTS = 96
NORMS = 208
CHUNK = 4096
SCORE_ROWS = 512
STAT_UNIT = 256
STAT_STEP = 256
VMEM_LIMIT = 24 << 20

SIN_COEFS = (3.14159258, -5.1677069, 2.55003164, -0.59804645, 0.07722225)
COS_COEFS = (0.99999995, -4.93479286, 4.05841191, -1.33188016, 0.21969679)


def horner(coefs, x):
    result = coefs[-1] * x + coefs[-2]
    for coef in coefs[-3::-1]:
        result = result * x + coef
    return result


def flat_lanes(rows):
    return jnp.concatenate([rows[c : c + 1] for c in range(rows.shape[0])], axis=1)


def candidate_kernel(
    coords_hbm, species_hbm, miller_hbm, offsets_hbm, amps_hbm, decay_hbm, refs_hbm,
    out_ref, refs_ref,
    coords_ref, species_ref, miller_ref, offsets_ref, amps_ref, decay_ref,
    grid_ref, spread_ref, sems,
):
    sources = (coords_hbm, species_hbm, amps_hbm, decay_hbm, miller_hbm, offsets_hbm, refs_hbm)
    targets = (coords_ref, species_ref, amps_ref, decay_ref, miller_ref, offsets_ref, refs_ref)
    copies = [
        pltpu.make_async_copy(source, target, sems.at[i])
        for i, (source, target) in enumerate(zip(sources, targets))
    ]
    for copy in copies:
        copy.start()
    f32, bf16 = jnp.float32, jnp.bfloat16
    count, atoms = species_ref.shape
    kinds = amps_ref.shape[1]
    reflections = miller_ref.shape[1]
    nbins = out_ref.shape[1]
    nblocks = nbins // LANES
    flat = count * atoms

    axis = lax.broadcasted_iota(jnp.int32, (9, 3 * LANES), 0) // 3
    column = lax.broadcasted_iota(jnp.int32, (9, 3 * LANES), 1)
    tile = column // LANES
    point = column - tile * LANES
    index1 = point // SIDE
    index2 = point - index1 * SIDE
    index2 = jnp.where(tile == 0, index2, -index2)
    yz = jnp.where(axis == 1, index1, jnp.where(axis == 2, index2, 0))
    indices = jnp.where(tile == 2, jnp.where(axis == 0, point, 0), yz)
    indices = indices.astype(f32).astype(bf16)

    point = lax.broadcasted_iota(jnp.int32, (NORMS, LANES), 1)
    index1 = point // SIDE
    index2 = point - index1 * SIDE
    rest = lax.broadcasted_iota(jnp.int32, (NORMS, LANES), 0) - index1 * index1 - index2 * index2
    pick = jnp.concatenate(
        [(rest == h0 * h0).astype(f32).astype(bf16) for h0 in range(SIDE)], axis=1
    )

    centre = lax.broadcasted_iota(jnp.int32, (LANES, 2 * LANES), 0)
    bins = lax.broadcasted_iota(jnp.int32, (LANES, 2 * LANES), 1)
    bins = jnp.where(bins < LANES + LANES // 2, bins, bins - 2 * LANES)
    distance = (bins - centre).astype(f32) * (1.0 / PEAK_WIDTH)
    profile = jnp.exp(-0.5 * distance * distance).astype(bf16)
    for copy in copies[:4]:
        copy.wait()
    pieces = []
    for axis in range(3):
        value = flat_lanes(coords_ref[axis])
        for _ in range(3):
            piece = value.astype(bf16)
            value = value - piece.astype(f32)
            pieces.append(piece.astype(f32))
    places = jnp.concatenate(pieces, axis=0).astype(bf16).T

    turns = jnp.dot(places, indices, preferred_element_type=f32)
    u = turns - jnp.round(turns)
    square = u * u
    half_sin = u * horner(SIN_COEFS, square)
    half_cos = horner(COS_COEFS, square)
    cosine = 1.0 - 2.0 * (half_sin * half_sin)
    sine = 2.0 * (half_sin * half_cos)

    norms = lax.broadcasted_iota(jnp.int32, (NORMS, kinds), 0).astype(f32) * Q_SCALE
    table = jnp.zeros((NORMS, kinds), f32)
    for term in range(amps_ref.shape[0]):
        table = table + amps_ref[term : term + 1, :] * jnp.exp(
            -decay_ref[term : term + 1, :] * norms
        )
    onehot = (
        lax.broadcasted_iota(jnp.int32, (kinds, flat), 0) == flat_lanes(species_ref[...])
    ).astype(f32).astype(bf16)
    atom_table = jnp.dot(
        table.astype(bf16), onehot, preferred_element_type=f32
    ).astype(bf16).T
    weight = jnp.dot(atom_table, pick, preferred_element_type=f32)

    points = 2 * SIDE * count
    for c in range(count):
        atom = slice(c * atoms, (c + 1) * atoms)
        for h0 in range(SIDE):
            w = weight[atom, h0 * LANES : (h0 + 1) * LANES]
            w_cos = w * cosine[atom, 2 * LANES + h0 : 2 * LANES + h0 + 1]
            w_sin = w * sine[atom, 2 * LANES + h0 : 2 * LANES + h0 + 1]
            for minus in range(2):
                cos12 = cosine[atom, minus * LANES : (minus + 1) * LANES]
                sin12 = sine[atom, minus * LANES : (minus + 1) * LANES]
                terms = (w_cos * cos12, w_sin * sin12, w_cos * sin12, w_sin * cos12)
                for i, term in enumerate(terms):
                    row = (i * points + (minus * SIDE + h0) * count + c) * 8
                    grid_ref[row : row + 8, :] = jnp.sum(term.reshape(-1, 8, LANES), axis=0)
    cc, ss, cs, sc = (
        sum(grid_ref[pl.ds(i * points * 8 + j, points, stride=8), :] for j in range(8))
        for i in range(4)
    )
    plus = (cc - ss) * (cc - ss) + (cs + sc) * (cs + sc)
    minus = (cc + ss) * (cc + ss) + (cs - sc) * (cs - sc)
    grid = jnp.concatenate([plus, minus], axis=0).astype(bf16)

    for copy in copies[4:6]:
        copy.wait()
    spread_ref[...] = jnp.zeros_like(spread_ref)

    def step(index, carry):
        cols = pl.ds(pl.multiple_of(index * CHUNK, CHUNK), CHUNK)
        miller = miller_ref[:, cols]
        miller = jnp.where(miller[1:2] < 0, -miller, miller)
        size = jnp.abs(miller)
        signs = jnp.where(miller < 0, 1, 0)
        place = size[1:2] * SIDE + size[2:3]
        chosen = (2 * signs[0:1] + signs[2:3]) * SIDE + size[0:1]
        at_place = (
            lax.broadcasted_iota(jnp.int32, (POINTS, CHUNK), 0) == place
        ).astype(f32).astype(bf16)
        values = jnp.dot(grid[:, :POINTS], at_place, preferred_element_type=f32)
        fold = lax.broadcasted_iota(jnp.int32, (8, CHUNK), 0) // count
        wanted = chosen - fold
        intensity = jnp.zeros((8, CHUNK), f32)
        for first in range(0, 4 * SIDE, 8 // count):
            rows = slice(first * count, first * count + 8)
            intensity = jnp.where(wanted == first, values[rows], intensity)
        shift = count
        while shift < 8:
            intensity = intensity + pltpu.roll(intensity, shift, axis=0)
            shift *= 2

        offset = offsets_ref[:, cols]
        block = offset // LANES
        fold = lax.broadcasted_iota(jnp.int32, (8, CHUNK), 0) // count
        routed = jnp.concatenate(
            [
                jnp.where(block == i + fold, intensity, 0.0)
                for i in range(0, nblocks, 8 // count)
            ],
            axis=0,
        ).astype(bf16)
        local = (
            lax.broadcasted_iota(jnp.int32, (LANES, CHUNK), 0) == offset - block * LANES
        ).astype(f32).astype(bf16)
        spread_ref[...] += lax.dot_general(
            local, routed, (((1,), (1,)), ((), ())), preferred_element_type=f32
        )
        return carry

    lax.fori_loop(0, reflections // CHUNK, step, 0, unroll=True)

    sums = spread_ref[...].T
    pieces = []
    for _ in range(3):
        pieces.append(sums.astype(bf16))
        sums = sums - pieces[-1].astype(f32)
    peaks = jnp.dot(
        jnp.concatenate(pieces, axis=1),
        jnp.concatenate([profile] * 3, axis=0),
        preferred_element_type=f32,
    )
    lane = lax.broadcasted_iota(jnp.int32, (count, LANES), 1)
    blocks = []
    for i in range(nblocks):
        own = peaks[i * count : (i + 1) * count, :LANES]
        before = after = jnp.zeros_like(own)
        if i > 0:
            before = peaks[(i - 1) * count : i * count, LANES:]
        if i + 1 < nblocks:
            after = peaks[(i + 1) * count : (i + 2) * count, LANES:]
        blocks.append(own + jnp.where(lane < LANES // 2, before, after))
    pattern = jnp.concatenate(blocks, axis=1)
    centered = pattern - jnp.mean(pattern, axis=1, keepdims=True)
    variance = jnp.mean(centered * centered, axis=1, keepdims=True)
    out_ref[...] = (centered / jnp.sqrt(variance + EPSILON)).astype(bf16)
    copies[-1].wait()


def candidate_patterns(coords, species, miller, offsets, form_amps, form_decay, refs):
    count, atoms = species.shape
    nbins = refs.shape[1]
    args = (coords, species, miller, offsets[None, :], form_amps.T, form_decay.T)
    args = [pltpu.with_memory_space_constraint(arg, pltpu.HBM) for arg in args + (refs,)]
    return pl.pallas_call(
        candidate_kernel,
        out_shape=[
            pltpu.VMEM((count, nbins), jnp.bfloat16),
            pltpu.VMEM(refs.shape, refs.dtype),
        ],
        in_specs=[pl.BlockSpec(memory_space=pltpu.HBM)] * len(args),
        scratch_shapes=[pltpu.VMEM(arg.shape, arg.dtype) for arg in args[:-1]]
        + [
            pltpu.VMEM((8 * 8 * SIDE * count + 8, LANES), jnp.float32),
            pltpu.VMEM((LANES, count * (nbins // LANES)), jnp.float32),
            pltpu.SemaphoreType.DMA((len(args),)),
        ],
        compiler_params=pltpu.CompilerParams(vmem_limit_bytes=VMEM_LIMIT),
        name="candidates",
    )(*args)


VMEM_WHOLE = pl.BlockSpec(memory_space=pltpu.VMEM)


def statistics_kernel(first, refs_ref, after_ref, mean_ref, scale_ref, same_ref):
    f32 = jnp.float32
    nbins = refs_ref.shape[1]
    rows = mean_ref.shape[0]
    for at in range(first, first + rows, STAT_STEP):
        tiles = [
            refs_ref[at : at + STAT_STEP, lane : lane + LANES].astype(f32)
            for lane in range(0, nbins, LANES)
        ]
        mean = jnp.sum(sum(tiles[1:], tiles[0]), axis=1, keepdims=True) * (1.0 / nbins)
        total = jnp.zeros((STAT_STEP, LANES), f32)
        for tile in tiles:
            total = total + (tile - mean) * (tile - mean)
        variance = jnp.sum(total, axis=1, keepdims=True) * (1.0 / nbins)
        mean_ref[at - first : at - first + STAT_STEP, :] = mean
        scale_ref[at - first : at - first + STAT_STEP, :] = lax.rsqrt(variance + EPSILON) * (1.0 / nbins**0.5)


def statistics(refs, first, rows, after):
    nbins = refs.shape[1]
    return pl.pallas_call(
        functools.partial(statistics_kernel, first),
        out_shape=[pltpu.VMEM((rows, 1), jnp.float32)] * 2 + [pltpu.VMEM(refs.shape, refs.dtype)],
        in_specs=[VMEM_WHOLE, pl.BlockSpec(memory_space=pl.ANY)],
        out_specs=[VMEM_WHOLE] * 3,
        input_output_aliases={0: 2},
        compiler_params=pltpu.CompilerParams(vmem_limit_bytes=VMEM_LIMIT),
        cost_estimate=pl.CostEstimate(
            flops=2 * rows * nbins * LANES, bytes_accessed=2 * rows * nbins, transcendentals=rows
        ),
        name="statistics",
    )(pltpu.with_memory_space_constraint(refs, pltpu.VMEM), after)


def score_kernel(ncand, masks, npieces, held_ref, other_ref, refs_ref, *rest):
    mean_refs, scale_refs = rest[:npieces], rest[npieces : 2 * npieces]
    out_ref, scores_ref, sems = rest[2 * npieces :]
    f32, bf16 = jnp.float32, jnp.bfloat16
    cand = jnp.concatenate([held_ref[...], other_ref[...]], axis=0)
    total, nbins = cand.shape
    block = total >> len(masks)
    last = (((1,), (1,)), ((), ()))
    place = lax.broadcasted_iota(jnp.int32, (total, total), 1)
    group = place // block
    position = lax.axis_index("db") * ncand + lax.axis_index("cand")
    source = jnp.full_like(group, position)
    for bit, mask in enumerate(masks):
        source = source ^ jnp.where((group >> bit) % 2 == 1, mask, 0)
    row = lax.broadcasted_iota(jnp.int32, (total, total), 0)
    order = (row == source * block + place % block).astype(f32).astype(bf16)
    cand = jnp.dot(order, cand, preferred_element_type=f32).astype(bf16)
    sums = lax.dot_general(jnp.ones((8, nbins), bf16), cand, last, preferred_element_type=f32)[:1]
    means, scales = (
        jnp.concatenate([ref[...] for ref in refs], axis=0) for refs in (mean_refs, scale_refs)
    )
    copies = []
    for i, start in enumerate(range(0, refs_ref.shape[0], SCORE_ROWS)):
        rows = slice(start, start + SCORE_ROWS)
        product = lax.dot_general(refs_ref[rows, :], cand, last, preferred_element_type=f32)
        product = (product - means[rows] * sums) * scales[rows]
        scores_ref[:, rows] = product.T.astype(bf16)
        copy = pltpu.make_async_copy(scores_ref.at[:, rows], out_ref.at[:, rows], sems.at[i])
        copy.start()
        copies.append(copy)
    for copy in copies:
        copy.wait()


def score(ncand, masks, held, other, refs, means, scales):
    total = held.shape[0] + other.shape[0]
    count = refs.shape[0]
    return pl.pallas_call(
        functools.partial(score_kernel, ncand, masks, len(means)),
        out_shape=jax.ShapeDtypeStruct((total, count), jnp.bfloat16),
        in_specs=[VMEM_WHOLE] * (3 + 2 * len(means)),
        out_specs=pl.BlockSpec(memory_space=pltpu.HBM),
        scratch_shapes=[
            pltpu.VMEM((total, count), jnp.bfloat16),
            pltpu.SemaphoreType.DMA((count // SCORE_ROWS,)),
        ],
        compiler_params=pltpu.CompilerParams(vmem_limit_bytes=VMEM_LIMIT),
        name="scores",
    )(held, other, pltpu.with_memory_space_constraint(refs, pltpu.VMEM), *means, *scales)


def per_device(ndb, ncand, coords, species, miller, offsets, form_amps, form_decay, ref_patterns):
    count, nbins = ref_patterns.shape
    held, refs = candidate_patterns(
        coords, species, miller, offsets, form_amps, form_decay, ref_patterns
    )
    members = ndb * ncand
    core = ncand
    masks = [core | 1 << bit for bit in reversed(range(ncand.bit_length() - 1))]
    masks += [core | ncand << bit for bit in range(1, ndb.bit_length() - 1)]
    masks.append(core)
    share = -(-count * 5 // 16 // STAT_UNIT) * STAT_UNIT
    means, scales = [], []
    first = 0
    for mask in masks:
        other = lax.ppermute(held, ("db", "cand"), [(i, i ^ mask) for i in range(members)])
        rows = min(share, count - first)
        if rows > 0:
            mean, scale, refs = statistics(refs, first, rows, held)
            means.append(mean)
            scales.append(scale)
            first += rows
            other, mean = lax.optimization_barrier((other, mean))
        if mask != core:
            held = jnp.concatenate([held, other], axis=0)
    if first < count:
        mean, scale, refs = statistics(refs, first, count - first, held)
        means.append(mean)
        scales.append(scale)
    return score(ncand, tuple(masks), held, other, refs, means, scales)


def solution(mesh):
    in_specs = (
        P(None, ("groups", "db", "cand"), None),
        P(("groups", "db", "cand"), None),
        P(),
        P(),
        P(),
        P(),
        P(("db", "cand"), None),
    )
    out_specs = P("groups", ("db", "cand"))
    body = functools.partial(per_device, mesh.shape["db"], mesh.shape["cand"])
    return jax.shard_map(
        body, mesh=mesh, in_specs=in_specs, out_specs=out_specs, check_vma=False
    )
```

```python
import functools

import jax
import jax.numpy as jnp
from jax import lax
from jax.experimental import pallas as pl
from jax.experimental.pallas import tpu as pltpu
from jax.sharding import PartitionSpec as P

EPSILON = 1e-06
Q_SCALE = 0.0025
PEAK_WIDTH = 0.5
LANES = 128
SIDE = 9
POINTS = 96
NORMS = 208
CHUNK = 4096
SCORE_ROWS = 512
STAT_UNIT = 256
STAT_STEP = 256
VMEM_LIMIT = 24 << 20

SIN_COEFS = (3.14159258, -5.1677069, 2.55003164, -0.59804645, 0.07722225)
COS_COEFS = (0.99999995, -4.93479286, 4.05841191, -1.33188016, 0.21969679)


def horner(coefs, x):
    result = coefs[-1] * x + coefs[-2]
    for coef in coefs[-3::-1]:
        result = result * x + coef
    return result


def flat_lanes(rows):
    return jnp.concatenate([rows[c : c + 1] for c in range(rows.shape[0])], axis=1)


def candidate_kernel(
    coords_hbm, species_hbm, miller_hbm, offsets_hbm, amps_hbm, decay_hbm, refs_hbm,
    out_ref, refs_ref,
    coords_ref, species_ref, miller_ref, offsets_ref, amps_ref, decay_ref,
    grid_ref, spread_ref, sems,
):
    sources = (coords_hbm, species_hbm, amps_hbm, decay_hbm, miller_hbm, offsets_hbm, refs_hbm)
    targets = (coords_ref, species_ref, amps_ref, decay_ref, miller_ref, offsets_ref, refs_ref)
    copies = [
        pltpu.make_async_copy(source, target, sems.at[i])
        for i, (source, target) in enumerate(zip(sources, targets))
    ]
    for copy in copies:
        copy.start()
    f32, bf16 = jnp.float32, jnp.bfloat16
    count, atoms = species_ref.shape
    kinds = amps_ref.shape[1]
    reflections = miller_ref.shape[1]
    nbins = out_ref.shape[1]
    nblocks = nbins // LANES
    flat = count * atoms

    axis = lax.broadcasted_iota(jnp.int32, (9, 3 * LANES), 0) // 3
    column = lax.broadcasted_iota(jnp.int32, (9, 3 * LANES), 1)
    tile = column // LANES
    point = column - tile * LANES
    index1 = point // SIDE
    index2 = point - index1 * SIDE
    index2 = jnp.where(tile == 0, index2, -index2)
    yz = jnp.where(axis == 1, index1, jnp.where(axis == 2, index2, 0))
    indices = jnp.where(tile == 2, jnp.where(axis == 0, point, 0), yz)
    indices = indices.astype(f32).astype(bf16)

    point = lax.broadcasted_iota(jnp.int32, (NORMS, LANES), 1)
    index1 = point // SIDE
    index2 = point - index1 * SIDE
    rest = lax.broadcasted_iota(jnp.int32, (NORMS, LANES), 0) - index1 * index1 - index2 * index2
    pick = jnp.concatenate(
        [(rest == h0 * h0).astype(f32).astype(bf16) for h0 in range(SIDE)], axis=1
    )

    centre = lax.broadcasted_iota(jnp.int32, (LANES, 2 * LANES), 0)
    bins = lax.broadcasted_iota(jnp.int32, (LANES, 2 * LANES), 1)
    bins = jnp.where(bins < LANES + LANES // 2, bins, bins - 2 * LANES)
    distance = (bins - centre).astype(f32) * (1.0 / PEAK_WIDTH)
    profile = jnp.exp(-0.5 * distance * distance).astype(bf16)
    for copy in copies[:4]:
        copy.wait()
    pieces = []
    for axis in range(3):
        value = flat_lanes(coords_ref[axis])
        for _ in range(3):
            piece = value.astype(bf16)
            value = value - piece.astype(f32)
            pieces.append(piece.astype(f32))
    places = jnp.concatenate(pieces, axis=0).astype(bf16).T

    turns = jnp.dot(places, indices, preferred_element_type=f32)
    u = turns - jnp.round(turns)
    square = u * u
    half_sin = u * horner(SIN_COEFS, square)
    half_cos = horner(COS_COEFS, square)
    cosine = 1.0 - 2.0 * (half_sin * half_sin)
    sine = 2.0 * (half_sin * half_cos)

    norms = lax.broadcasted_iota(jnp.int32, (NORMS, kinds), 0).astype(f32) * Q_SCALE
    table = jnp.zeros((NORMS, kinds), f32)
    for term in range(amps_ref.shape[0]):
        table = table + amps_ref[term : term + 1, :] * jnp.exp(
            -decay_ref[term : term + 1, :] * norms
        )
    onehot = (
        lax.broadcasted_iota(jnp.int32, (kinds, flat), 0) == flat_lanes(species_ref[...])
    ).astype(f32).astype(bf16)
    atom_table = jnp.dot(
        table.astype(bf16), onehot, preferred_element_type=f32
    ).astype(bf16).T
    weight = jnp.dot(atom_table, pick, preferred_element_type=f32)

    points = 2 * SIDE * count
    for c in range(count):
        atom = slice(c * atoms, (c + 1) * atoms)
        for h0 in range(SIDE):
            w = weight[atom, h0 * LANES : (h0 + 1) * LANES]
            w_cos = w * cosine[atom, 2 * LANES + h0 : 2 * LANES + h0 + 1]
            w_sin = w * sine[atom, 2 * LANES + h0 : 2 * LANES + h0 + 1]
            for minus in range(2):
                cos12 = cosine[atom, minus * LANES : (minus + 1) * LANES]
                sin12 = sine[atom, minus * LANES : (minus + 1) * LANES]
                terms = (w_cos * cos12, w_sin * sin12, w_cos * sin12, w_sin * cos12)
                for i, term in enumerate(terms):
                    row = (i * points + (minus * SIDE + h0) * count + c) * 8
                    grid_ref[row : row + 8, :] = jnp.sum(term.reshape(-1, 8, LANES), axis=0)
    cc, ss, cs, sc = (
        sum(grid_ref[pl.ds(i * points * 8 + j, points, stride=8), :] for j in range(8))
        for i in range(4)
    )
    plus = (cc - ss) * (cc - ss) + (cs + sc) * (cs + sc)
    minus = (cc + ss) * (cc + ss) + (cs - sc) * (cs - sc)
    grid = jnp.concatenate([plus, minus], axis=0).astype(bf16)

    for copy in copies[4:6]:
        copy.wait()
    spread_ref[...] = jnp.zeros_like(spread_ref)

    def step(index, carry):
        cols = pl.ds(pl.multiple_of(index * CHUNK, CHUNK), CHUNK)
        miller = miller_ref[:, cols]
        miller = jnp.where(miller[1:2] < 0, -miller, miller)
        size = jnp.abs(miller)
        signs = jnp.where(miller < 0, 1, 0)
        place = size[1:2] * SIDE + size[2:3]
        chosen = (2 * signs[0:1] + signs[2:3]) * SIDE + size[0:1]
        at_place = (
            lax.broadcasted_iota(jnp.int32, (POINTS, CHUNK), 0) == place
        ).astype(f32).astype(bf16)
        values = jnp.dot(grid[:, :POINTS], at_place, preferred_element_type=f32)
        fold = lax.broadcasted_iota(jnp.int32, (8, CHUNK), 0) // count
        wanted = chosen - fold
        intensity = jnp.zeros((8, CHUNK), f32)
        for first in range(0, 4 * SIDE, 8 // count):
            rows = slice(first * count, first * count + 8)
            intensity = jnp.where(wanted == first, values[rows], intensity)
        shift = count
        while shift < 8:
            intensity = intensity + pltpu.roll(intensity, shift, axis=0)
            shift *= 2

        offset = offsets_ref[:, cols]
        block = offset // LANES
        fold = lax.broadcasted_iota(jnp.int32, (8, CHUNK), 0) // count
        routed = jnp.concatenate(
            [
                jnp.where(block == i + fold, intensity, 0.0)
                for i in range(0, nblocks, 8 // count)
            ],
            axis=0,
        ).astype(bf16)
        local = (
            lax.broadcasted_iota(jnp.int32, (LANES, CHUNK), 0) == offset - block * LANES
        ).astype(f32).astype(bf16)
        spread_ref[...] += lax.dot_general(
            local, routed, (((1,), (1,)), ((), ())), preferred_element_type=f32
        )
        return carry

    lax.fori_loop(0, reflections // CHUNK, step, 0, unroll=True)

    sums = spread_ref[...].T
    pieces = []
    for _ in range(3):
        pieces.append(sums.astype(bf16))
        sums = sums - pieces[-1].astype(f32)
    peaks = jnp.dot(
        jnp.concatenate(pieces, axis=1),
        jnp.concatenate([profile] * 3, axis=0),
        preferred_element_type=f32,
    )
    lane = lax.broadcasted_iota(jnp.int32, (count, LANES), 1)
    blocks = []
    for i in range(nblocks):
        own = peaks[i * count : (i + 1) * count, :LANES]
        before = after = jnp.zeros_like(own)
        if i > 0:
            before = peaks[(i - 1) * count : i * count, LANES:]
        if i + 1 < nblocks:
            after = peaks[(i + 1) * count : (i + 2) * count, LANES:]
        blocks.append(own + jnp.where(lane < LANES // 2, before, after))
    pattern = jnp.concatenate(blocks, axis=1)
    centered = pattern - jnp.mean(pattern, axis=1, keepdims=True)
    variance = jnp.mean(centered * centered, axis=1, keepdims=True)
    out_ref[...] = (centered / jnp.sqrt(variance + EPSILON)).astype(bf16)
    copies[-1].wait()


def candidate_patterns(coords, species, miller, offsets, form_amps, form_decay, refs):
    count, atoms = species.shape
    nbins = refs.shape[1]
    args = (coords, species, miller, offsets[None, :], form_amps.T, form_decay.T)
    args = [pltpu.with_memory_space_constraint(arg, pltpu.HBM) for arg in args + (refs,)]
    return pl.pallas_call(
        candidate_kernel,
        out_shape=[
            pltpu.VMEM((count, nbins), jnp.bfloat16),
            pltpu.VMEM(refs.shape, refs.dtype),
        ],
        in_specs=[pl.BlockSpec(memory_space=pltpu.HBM)] * len(args),
        scratch_shapes=[pltpu.VMEM(arg.shape, arg.dtype) for arg in args[:-1]]
        + [
            pltpu.VMEM((8 * 8 * SIDE * count + 8, LANES), jnp.float32),
            pltpu.VMEM((LANES, count * (nbins // LANES)), jnp.float32),
            pltpu.SemaphoreType.DMA((len(args),)),
        ],
        compiler_params=pltpu.CompilerParams(vmem_limit_bytes=VMEM_LIMIT),
        name="candidates",
    )(*args)


VMEM_WHOLE = pl.BlockSpec(memory_space=pltpu.VMEM)


def statistics_kernel(first, refs_ref, after_ref, mean_ref, scale_ref, same_ref):
    f32 = jnp.float32
    nbins = refs_ref.shape[1]
    rows = mean_ref.shape[0]
    for at in range(first, first + rows, STAT_STEP):
        tiles = [
            refs_ref[at : at + STAT_STEP, lane : lane + LANES].astype(f32)
            for lane in range(0, nbins, LANES)
        ]
        mean = jnp.sum(sum(tiles[1:], tiles[0]), axis=1, keepdims=True) * (1.0 / nbins)
        total = jnp.zeros((STAT_STEP, LANES), f32)
        for tile in tiles:
            total = total + (tile - mean) * (tile - mean)
        variance = jnp.sum(total, axis=1, keepdims=True) * (1.0 / nbins)
        mean_ref[at - first : at - first + STAT_STEP, :] = mean
        scale_ref[at - first : at - first + STAT_STEP, :] = lax.rsqrt(variance + EPSILON) * (1.0 / nbins**0.5)


def statistics(refs, first, rows, after):
    nbins = refs.shape[1]
    return pl.pallas_call(
        functools.partial(statistics_kernel, first),
        out_shape=[pltpu.VMEM((rows, 1), jnp.float32)] * 2 + [pltpu.VMEM(refs.shape, refs.dtype)],
        in_specs=[VMEM_WHOLE, pl.BlockSpec(memory_space=pl.ANY)],
        out_specs=[VMEM_WHOLE] * 3,
        input_output_aliases={0: 2},
        compiler_params=pltpu.CompilerParams(vmem_limit_bytes=VMEM_LIMIT),
        cost_estimate=pl.CostEstimate(
            flops=2 * rows * nbins * LANES, bytes_accessed=2 * rows * nbins, transcendentals=rows
        ),
        name="statistics",
    )(pltpu.with_memory_space_constraint(refs, pltpu.VMEM), after)


def score_kernel(ncand, masks, npieces, held_ref, other_ref, refs_ref, *rest):
    mean_refs, scale_refs = rest[:npieces], rest[npieces : 2 * npieces]
    out_ref, scores_ref, sems = rest[2 * npieces :]
    f32, bf16 = jnp.float32, jnp.bfloat16
    cand = jnp.concatenate([held_ref[...], other_ref[...]], axis=0)
    total, nbins = cand.shape
    block = total >> len(masks)
    last = (((1,), (1,)), ((), ()))
    place = lax.broadcasted_iota(jnp.int32, (total, total), 1)
    group = place // block
    position = lax.axis_index("db") * ncand + lax.axis_index("cand")
    source = jnp.full_like(group, position)
    for bit, mask in enumerate(masks):
        source = source ^ jnp.where((group >> bit) % 2 == 1, mask, 0)
    row = lax.broadcasted_iota(jnp.int32, (total, total), 0)
    order = (row == source * block + place % block).astype(f32).astype(bf16)
    cand = jnp.dot(order, cand, preferred_element_type=f32).astype(bf16)
    sums = lax.dot_general(jnp.ones((8, nbins), bf16), cand, last, preferred_element_type=f32)[:1]
    means, scales = (
        jnp.concatenate([ref[...] for ref in refs], axis=0) for refs in (mean_refs, scale_refs)
    )
    copies = []
    for i, start in enumerate(range(0, refs_ref.shape[0], SCORE_ROWS)):
        rows = slice(start, start + SCORE_ROWS)
        product = lax.dot_general(refs_ref[rows, :], cand, last, preferred_element_type=f32)
        product = (product - means[rows] * sums) * scales[rows]
        scores_ref[:, rows] = product.T.astype(bf16)
        copy = pltpu.make_async_copy(scores_ref.at[:, rows], out_ref.at[:, rows], sems.at[i])
        copy.start()
        copies.append(copy)
    for copy in copies:
        copy.wait()


def score(ncand, masks, held, other, refs, means, scales):
    total = held.shape[0] + other.shape[0]
    count = refs.shape[0]
    return pl.pallas_call(
        functools.partial(score_kernel, ncand, masks, len(means)),
        out_shape=jax.ShapeDtypeStruct((total, count), jnp.bfloat16),
        in_specs=[VMEM_WHOLE] * (3 + 2 * len(means)),
        out_specs=pl.BlockSpec(memory_space=pltpu.HBM),
        scratch_shapes=[
            pltpu.VMEM((total, count), jnp.bfloat16),
            pltpu.SemaphoreType.DMA((count // SCORE_ROWS,)),
        ],
        compiler_params=pltpu.CompilerParams(vmem_limit_bytes=VMEM_LIMIT),
        name="scores",
    )(held, other, pltpu.with_memory_space_constraint(refs, pltpu.VMEM), *means, *scales)


def per_device(ndb, ncand, coords, species, miller, offsets, form_amps, form_decay, ref_patterns):
    count, nbins = ref_patterns.shape
    held, refs = candidate_patterns(
        coords, species, miller, offsets, form_amps, form_decay, ref_patterns
    )
    members = ndb * ncand
    core = ncand
    masks = [core | 1 << bit for bit in reversed(range(ncand.bit_length() - 1))]
    masks += [core | ncand << bit for bit in range(1, ndb.bit_length() - 1)]
    masks.append(core)
    share = -(-count * 5 // 16 // STAT_UNIT) * STAT_UNIT
    means, scales = [], []
    first = 0
    for stage, mask in enumerate(masks):
        other = lax.ppermute(held, ("db", "cand"), [(i, i ^ mask) for i in range(members)])
        rows = min(share, count - first)
        if stage == len(masks) - 2:
            rows = count - first
        if rows > 0:
            mean, scale, refs = statistics(refs, first, rows, held)
            means.append(mean)
            scales.append(scale)
            first += rows
            other, mean = lax.optimization_barrier((other, mean))
        if mask != core:
            held = jnp.concatenate([held, other], axis=0)
    if first < count:
        mean, scale, refs = statistics(refs, first, count - first, held)
        means.append(mean)
        scales.append(scale)
    return score(ncand, tuple(masks), held, other, refs, means, scales)


def solution(mesh):
    in_specs = (
        P(None, ("groups", "db", "cand"), None),
        P(("groups", "db", "cand"), None),
        P(),
        P(),
        P(),
        P(),
        P(("db", "cand"), None),
    )
    out_specs = P("groups", ("db", "cand"))
    body = functools.partial(per_device, mesh.shape["db"], mesh.shape["cand"])
    return jax.shard_map(
        body, mesh=mesh, in_specs=in_specs, out_specs=out_specs, check_vma=False
    )
```

```python
import functools

import jax
import jax.numpy as jnp
from jax import lax
from jax.experimental import pallas as pl
from jax.experimental.pallas import tpu as pltpu
from jax.sharding import PartitionSpec as P

EPSILON = 1e-06
Q_SCALE = 0.0025
PEAK_WIDTH = 0.5
LANES = 128
SIDE = 9
POINTS = 96
NORMS = 208
CHUNK = 2048
SCORE_ROWS = 512
STAT_UNIT = 256
STAT_STEP = 256
VMEM_LIMIT = 24 << 20

SIN_COEFS = (3.14159258, -5.1677069, 2.55003164, -0.59804645, 0.07722225)
COS_COEFS = (0.99999995, -4.93479286, 4.05841191, -1.33188016, 0.21969679)


def horner(coefs, x):
    result = coefs[-1] * x + coefs[-2]
    for coef in coefs[-3::-1]:
        result = result * x + coef
    return result


def flat_lanes(rows):
    return jnp.concatenate([rows[c : c + 1] for c in range(rows.shape[0])], axis=1)


def candidate_kernel(
    coords_hbm, species_hbm, miller_hbm, offsets_hbm, amps_hbm, decay_hbm, refs_hbm,
    out_ref, refs_ref,
    coords_ref, species_ref, miller_ref, offsets_ref, amps_ref, decay_ref,
    grid_ref, spread_ref, sems,
):
    sources = (coords_hbm, species_hbm, amps_hbm, decay_hbm, miller_hbm, offsets_hbm, refs_hbm)
    targets = (coords_ref, species_ref, amps_ref, decay_ref, miller_ref, offsets_ref, refs_ref)
    copies = [
        pltpu.make_async_copy(source, target, sems.at[i])
        for i, (source, target) in enumerate(zip(sources, targets))
    ]
    for copy in copies:
        copy.start()
    f32, bf16 = jnp.float32, jnp.bfloat16
    count, atoms = species_ref.shape
    kinds = amps_ref.shape[1]
    reflections = miller_ref.shape[1]
    nbins = out_ref.shape[1]
    nblocks = nbins // LANES
    flat = count * atoms

    axis = lax.broadcasted_iota(jnp.int32, (9, 3 * LANES), 0) // 3
    column = lax.broadcasted_iota(jnp.int32, (9, 3 * LANES), 1)
    tile = column // LANES
    point = column - tile * LANES
    index1 = point // SIDE
    index2 = point - index1 * SIDE
    index2 = jnp.where(tile == 0, index2, -index2)
    yz = jnp.where(axis == 1, index1, jnp.where(axis == 2, index2, 0))
    indices = jnp.where(tile == 2, jnp.where(axis == 0, point, 0), yz)
    indices = indices.astype(f32).astype(bf16)

    point = lax.broadcasted_iota(jnp.int32, (NORMS, LANES), 1)
    index1 = point // SIDE
    index2 = point - index1 * SIDE
    rest = lax.broadcasted_iota(jnp.int32, (NORMS, LANES), 0) - index1 * index1 - index2 * index2
    pick = jnp.concatenate(
        [(rest == h0 * h0).astype(f32).astype(bf16) for h0 in range(SIDE)], axis=1
    )

    centre = lax.broadcasted_iota(jnp.int32, (LANES, 2 * LANES), 0)
    bins = lax.broadcasted_iota(jnp.int32, (LANES, 2 * LANES), 1)
    bins = jnp.where(bins < LANES + LANES // 2, bins, bins - 2 * LANES)
    distance = (bins - centre).astype(f32) * (1.0 / PEAK_WIDTH)
    profile = jnp.exp(-0.5 * distance * distance).astype(bf16)
    for copy in copies[:4]:
        copy.wait()
    pieces = []
    for axis in range(3):
        value = flat_lanes(coords_ref[axis])
        for _ in range(3):
            piece = value.astype(bf16)
            value = value - piece.astype(f32)
            pieces.append(piece.astype(f32))
    places = jnp.concatenate(pieces, axis=0).astype(bf16).T

    turns = jnp.dot(places, indices, preferred_element_type=f32)
    u = turns - jnp.round(turns)
    square = u * u
    half_sin = u * horner(SIN_COEFS, square)
    half_cos = horner(COS_COEFS, square)
    cosine = 1.0 - 2.0 * (half_sin * half_sin)
    sine = 2.0 * (half_sin * half_cos)

    norms = lax.broadcasted_iota(jnp.int32, (NORMS, kinds), 0).astype(f32) * Q_SCALE
    table = jnp.zeros((NORMS, kinds), f32)
    for term in range(amps_ref.shape[0]):
        table = table + amps_ref[term : term + 1, :] * jnp.exp(
            -decay_ref[term : term + 1, :] * norms
        )
    onehot = (
        lax.broadcasted_iota(jnp.int32, (kinds, flat), 0) == flat_lanes(species_ref[...])
    ).astype(f32).astype(bf16)
    atom_table = jnp.dot(
        table.astype(bf16), onehot, preferred_element_type=f32
    ).astype(bf16).T
    weight = jnp.dot(atom_table, pick, preferred_element_type=f32)

    points = 2 * SIDE * count
    for c in range(count):
        atom = slice(c * atoms, (c + 1) * atoms)
        for h0 in range(SIDE):
            w = weight[atom, h0 * LANES : (h0 + 1) * LANES]
            w_cos = w * cosine[atom, 2 * LANES + h0 : 2 * LANES + h0 + 1]
            w_sin = w * sine[atom, 2 * LANES + h0 : 2 * LANES + h0 + 1]
            for minus in range(2):
                cos12 = cosine[atom, minus * LANES : (minus + 1) * LANES]
                sin12 = sine[atom, minus * LANES : (minus + 1) * LANES]
                terms = (w_cos * cos12, w_sin * sin12, w_cos * sin12, w_sin * cos12)
                for i, term in enumerate(terms):
                    row = (i * points + (minus * SIDE + h0) * count + c) * 8
                    grid_ref[row : row + 8, :] = jnp.sum(term.reshape(-1, 8, LANES), axis=0)
    cc, ss, cs, sc = (
        sum(grid_ref[pl.ds(i * points * 8 + j, points, stride=8), :] for j in range(8))
        for i in range(4)
    )
    plus = (cc - ss) * (cc - ss) + (cs + sc) * (cs + sc)
    minus = (cc + ss) * (cc + ss) + (cs - sc) * (cs - sc)
    grid = jnp.concatenate([plus, minus], axis=0).astype(bf16)

    for copy in copies[4:6]:
        copy.wait()
    spread_ref[...] = jnp.zeros_like(spread_ref)

    def step(index, carry):
        cols = pl.ds(pl.multiple_of(index * CHUNK, CHUNK), CHUNK)
        miller = miller_ref[:, cols]
        miller = jnp.where(miller[1:2] < 0, -miller, miller)
        size = jnp.abs(miller)
        signs = jnp.where(miller < 0, 1, 0)
        place = size[1:2] * SIDE + size[2:3]
        chosen = (2 * signs[0:1] + signs[2:3]) * SIDE + size[0:1]
        at_place = (
            lax.broadcasted_iota(jnp.int32, (POINTS, CHUNK), 0) == place
        ).astype(f32).astype(bf16)
        values = jnp.dot(grid[:, :POINTS], at_place, preferred_element_type=f32)
        fold = lax.broadcasted_iota(jnp.int32, (8, CHUNK), 0) // count
        wanted = chosen - fold
        intensity = jnp.zeros((8, CHUNK), f32)
        for first in range(0, 4 * SIDE, 8 // count):
            rows = slice(first * count, first * count + 8)
            intensity = jnp.where(wanted == first, values[rows], intensity)
        shift = count
        while shift < 8:
            intensity = intensity + pltpu.roll(intensity, shift, axis=0)
            shift *= 2

        offset = offsets_ref[:, cols]
        block = offset // LANES
        fold = lax.broadcasted_iota(jnp.int32, (8, CHUNK), 0) // count
        routed = jnp.concatenate(
            [
                jnp.where(block == i + fold, intensity, 0.0)
                for i in range(0, nblocks, 8 // count)
            ],
            axis=0,
        ).astype(bf16)
        local = (
            lax.broadcasted_iota(jnp.int32, (LANES, CHUNK), 0) == offset - block * LANES
        ).astype(f32).astype(bf16)
        spread_ref[...] += lax.dot_general(
            local, routed, (((1,), (1,)), ((), ())), preferred_element_type=f32
        )
        return carry

    lax.fori_loop(0, reflections // CHUNK, step, 0, unroll=True)

    sums = spread_ref[...].T
    pieces = []
    for _ in range(3):
        pieces.append(sums.astype(bf16))
        sums = sums - pieces[-1].astype(f32)
    peaks = jnp.dot(
        jnp.concatenate(pieces, axis=1),
        jnp.concatenate([profile] * 3, axis=0),
        preferred_element_type=f32,
    )
    lane = lax.broadcasted_iota(jnp.int32, (count, LANES), 1)
    blocks = []
    for i in range(nblocks):
        own = peaks[i * count : (i + 1) * count, :LANES]
        before = after = jnp.zeros_like(own)
        if i > 0:
            before = peaks[(i - 1) * count : i * count, LANES:]
        if i + 1 < nblocks:
            after = peaks[(i + 1) * count : (i + 2) * count, LANES:]
        blocks.append(own + jnp.where(lane < LANES // 2, before, after))
    pattern = jnp.concatenate(blocks, axis=1)
    centered = pattern - jnp.mean(pattern, axis=1, keepdims=True)
    variance = jnp.mean(centered * centered, axis=1, keepdims=True)
    out_ref[...] = (centered / jnp.sqrt(variance + EPSILON)).astype(bf16)
    copies[-1].wait()


def candidate_patterns(coords, species, miller, offsets, form_amps, form_decay, refs):
    count, atoms = species.shape
    nbins = refs.shape[1]
    args = (coords, species, miller, offsets[None, :], form_amps.T, form_decay.T)
    args = [pltpu.with_memory_space_constraint(arg, pltpu.HBM) for arg in args + (refs,)]
    return pl.pallas_call(
        candidate_kernel,
        out_shape=[
            pltpu.VMEM((count, nbins), jnp.bfloat16),
            pltpu.VMEM(refs.shape, refs.dtype),
        ],
        in_specs=[pl.BlockSpec(memory_space=pltpu.HBM)] * len(args),
        scratch_shapes=[pltpu.VMEM(arg.shape, arg.dtype) for arg in args[:-1]]
        + [
            pltpu.VMEM((8 * 8 * SIDE * count + 8, LANES), jnp.float32),
            pltpu.VMEM((LANES, count * (nbins // LANES)), jnp.float32),
            pltpu.SemaphoreType.DMA((len(args),)),
        ],
        compiler_params=pltpu.CompilerParams(vmem_limit_bytes=VMEM_LIMIT),
        name="candidates",
    )(*args)


VMEM_WHOLE = pl.BlockSpec(memory_space=pltpu.VMEM)


def statistics_kernel(first, refs_ref, after_ref, mean_ref, scale_ref, same_ref):
    f32 = jnp.float32
    nbins = refs_ref.shape[1]
    rows = mean_ref.shape[0]
    for at in range(first, first + rows, STAT_STEP):
        tiles = [
            refs_ref[at : at + STAT_STEP, lane : lane + LANES].astype(f32)
            for lane in range(0, nbins, LANES)
        ]
        mean = jnp.sum(sum(tiles[1:], tiles[0]), axis=1, keepdims=True) * (1.0 / nbins)
        total = jnp.zeros((STAT_STEP, LANES), f32)
        for tile in tiles:
            total = total + (tile - mean) * (tile - mean)
        variance = jnp.sum(total, axis=1, keepdims=True) * (1.0 / nbins)
        mean_ref[at - first : at - first + STAT_STEP, :] = mean
        scale_ref[at - first : at - first + STAT_STEP, :] = lax.rsqrt(variance + EPSILON) * (1.0 / nbins**0.5)


def statistics(refs, first, rows, after):
    nbins = refs.shape[1]
    return pl.pallas_call(
        functools.partial(statistics_kernel, first),
        out_shape=[pltpu.VMEM((rows, 1), jnp.float32)] * 2 + [pltpu.VMEM(refs.shape, refs.dtype)],
        in_specs=[VMEM_WHOLE, pl.BlockSpec(memory_space=pl.ANY)],
        out_specs=[VMEM_WHOLE] * 3,
        input_output_aliases={0: 2},
        compiler_params=pltpu.CompilerParams(vmem_limit_bytes=VMEM_LIMIT),
        cost_estimate=pl.CostEstimate(
            flops=2 * rows * nbins * LANES, bytes_accessed=2 * rows * nbins, transcendentals=rows
        ),
        name="statistics",
    )(pltpu.with_memory_space_constraint(refs, pltpu.VMEM), after)


def score_kernel(ncand, masks, npieces, held_ref, other_ref, refs_ref, *rest):
    mean_refs, scale_refs = rest[:npieces], rest[npieces : 2 * npieces]
    out_ref, scores_ref, sems = rest[2 * npieces :]
    f32, bf16 = jnp.float32, jnp.bfloat16
    cand = jnp.concatenate([held_ref[...], other_ref[...]], axis=0)
    total, nbins = cand.shape
    block = total >> len(masks)
    last = (((1,), (1,)), ((), ()))
    place = lax.broadcasted_iota(jnp.int32, (total, total), 1)
    group = place // block
    position = lax.axis_index("db") * ncand + lax.axis_index("cand")
    source = jnp.full_like(group, position)
    for bit, mask in enumerate(masks):
        source = source ^ jnp.where((group >> bit) % 2 == 1, mask, 0)
    row = lax.broadcasted_iota(jnp.int32, (total, total), 0)
    order = (row == source * block + place % block).astype(f32).astype(bf16)
    cand = jnp.dot(order, cand, preferred_element_type=f32).astype(bf16)
    sums = lax.dot_general(jnp.ones((8, nbins), bf16), cand, last, preferred_element_type=f32)[:1]
    means, scales = (
        jnp.concatenate([ref[...] for ref in refs], axis=0) for refs in (mean_refs, scale_refs)
    )
    copies = []
    for i, start in enumerate(range(0, refs_ref.shape[0], SCORE_ROWS)):
        rows = slice(start, start + SCORE_ROWS)
        product = lax.dot_general(refs_ref[rows, :], cand, last, preferred_element_type=f32)
        product = (product - means[rows] * sums) * scales[rows]
        scores_ref[:, rows] = product.T.astype(bf16)
        copy = pltpu.make_async_copy(scores_ref.at[:, rows], out_ref.at[:, rows], sems.at[i])
        copy.start()
        copies.append(copy)
    for copy in copies:
        copy.wait()


def score(ncand, masks, held, other, refs, means, scales):
    total = held.shape[0] + other.shape[0]
    count = refs.shape[0]
    return pl.pallas_call(
        functools.partial(score_kernel, ncand, masks, len(means)),
        out_shape=jax.ShapeDtypeStruct((total, count), jnp.bfloat16),
        in_specs=[VMEM_WHOLE] * (3 + 2 * len(means)),
        out_specs=pl.BlockSpec(memory_space=pltpu.HBM),
        scratch_shapes=[
            pltpu.VMEM((total, count), jnp.bfloat16),
            pltpu.SemaphoreType.DMA((count // SCORE_ROWS,)),
        ],
        compiler_params=pltpu.CompilerParams(vmem_limit_bytes=VMEM_LIMIT),
        name="scores",
    )(held, other, pltpu.with_memory_space_constraint(refs, pltpu.VMEM), *means, *scales)


def per_device(ndb, ncand, coords, species, miller, offsets, form_amps, form_decay, ref_patterns):
    count, nbins = ref_patterns.shape
    held, refs = candidate_patterns(
        coords, species, miller, offsets, form_amps, form_decay, ref_patterns
    )
    members = ndb * ncand
    core = ncand
    masks = [core | 1 << bit for bit in reversed(range(ncand.bit_length() - 1))]
    masks += [core | ncand << bit for bit in range(1, ndb.bit_length() - 1)]
    masks.append(core)
    share = -(-count * 5 // 16 // STAT_UNIT) * STAT_UNIT
    means, scales = [], []
    first = 0
    for stage, mask in enumerate(masks):
        other = lax.ppermute(held, ("db", "cand"), [(i, i ^ mask) for i in range(members)])
        rows = min(share, count - first)
        if stage == len(masks) - 2:
            rows = count - first
        if rows > 0:
            mean, scale, refs = statistics(refs, first, rows, held)
            means.append(mean)
            scales.append(scale)
            first += rows
            other, mean = lax.optimization_barrier((other, mean))
        if mask != core:
            held = jnp.concatenate([held, other], axis=0)
    if first < count:
        mean, scale, refs = statistics(refs, first, count - first, held)
        means.append(mean)
        scales.append(scale)
    return score(ncand, tuple(masks), held, other, refs, means, scales)


def solution(mesh):
    in_specs = (
        P(None, ("groups", "db", "cand"), None),
        P(("groups", "db", "cand"), None),
        P(),
        P(),
        P(),
        P(),
        P(("db", "cand"), None),
    )
    out_specs = P("groups", ("db", "cand"))
    body = functools.partial(per_device, mesh.shape["db"], mesh.shape["cand"])
    return jax.shard_map(
        body, mesh=mesh, in_specs=in_specs, out_specs=out_specs, check_vma=False
    )
```
